32 devices in a mesh: field: 2 (over x), soil: 4 (over y, core), stand: 4 (over z).
Axes of the slice: x: 2, y: 2, z: 4, core: 2. Of those that a mesh axis runs over, the one named last changes fastest.
Arguments:
- query_tokens: bfloat16 [4096, 1024], P(('field', 'stand', 'soil')), parts along dimension 0, may hold values from -80 to 80
- key_tokens: bfloat16 [4096, 1024], P(('field', 'soil')), parts along dimension 0, may hold values from -6 to 6
- w_in: bfloat16 [1024, 1536], replicated, may hold values from -0.1875 to 0.1875
- w_out: bfloat16 [512, 1024], replicated, may hold values from -0.25 to 0.25
- out_grad: bfloat16 [4096, 1024], P(('field', 'stand', 'soil')), parts along dimension 0, may hold values from -6 to 6
- crossing: int32 [32, 16], P(('field', 'stand', 'soil')), parts along dimension 0, may hold values from 0 to 1
- home: int32 [32], P(('field', 'stand', 'soil')), parts along dimension 0, may hold values from 0 to 15
Outputs:
- output: bfloat16 [4096, 1024], P(('field', 'stand', 'soil')), parts along dimension 0
- query_grad: bfloat16 [4096, 1024], P(('field', 'stand', 'soil')), parts along dimension 0
- key_grad: bfloat16 [4096, 1024], P(('field', 'soil')), parts along dimension 0
- w_in_grad: float32 [2048, 1536], P(('field', 'soil')), parts along dimension 0
- w_out_grad: float32 [1024, 1024], P(('field', 'soil')), parts along dimension 0
The draws below stay inside these ranges and needn't reach their ends.
There are 2 independent parts, one for each index of `field`. The reference program is written for one: setup_inputs(seed, part) draws one part's arguments, and reference() takes and returns one part's arrays. A program takes and returns all parts, laid end to end along the dimension named above; an argument that names none is the same for every part. Nothing has to cross between parts.
All inputs are finite; a program needn't handle non-finite values.
Results may differ from the reference program's by a relative error of at most 0.039.
Values may be sent and summed in bfloat16 or wider, within the bound.
No kernel may reach another device: no remote copies, remote signals or barrier semaphores. Data moves between devices by JAX's collectives and lax.ppermute only.
A program may use at most 128 MiB of HBM per device.

```python
import math
import jax
import jax.numpy as jnp
from jax import lax

D = 1024
HEADS = 4
DH = 128
BLOCK = 128
QUERIES = 2048
KEYS = 2048
QB = 16
KB = 16


def draw_crossing(key, part):
    level = jax.random.randint(jax.random.fold_in(key, 11), (QB, 1), 0, 5)
    cells = jax.random.randint(jax.random.fold_in(key, 12), (QB, KB), 0, 8)
    return (cells < level * 2).astype(jnp.int32)


def draw_query_tokens(key, part):
    base = jnp.clip(jax.random.normal(key, (QUERIES, D), jnp.float32), -6.0, 6.0)
    return base.astype(jnp.bfloat16)


def set_ends(entries, own_key, least, top_value):
    index_at = [jax.random.randint(jax.random.fold_in(own_key, axis), (), 0, length) for axis, length in enumerate(entries.shape)]
    main_axis = entries.shape.index(max(entries.shape))
    next_to = index_at[:main_axis] + [(index_at[main_axis] + 1) % entries.shape[main_axis]] + index_at[main_axis + 1:]
    return entries.at[tuple(index_at)].set(least).at[tuple(next_to)].set(top_value)


def block_scale(key, extent, cuts, low, high):
    level, own = 1.0, jax.random.fold_in(key, 6)
    for axis_at, parts in cuts:
        heights = jnp.exp(jax.random.uniform(jax.random.fold_in(own, axis_at), (parts,), jnp.float32, low / len(cuts), high / len(cuts)))
        level = level * jnp.repeat(heights, extent[axis_at] // parts).reshape([-1 if axis == axis_at else 1 for axis in range(len(extent))])
    return level


def centred(rng, extent, scale, bound, pieces=(), held_as=jnp.bfloat16):
    factor_of = block_scale(rng, extent, pieces, -0.22, 0.18) if pieces else 1.0
    values = jax.random.normal(rng, extent, jnp.float32) * scale * factor_of
    return jnp.minimum(jnp.maximum(values, -bound), bound).astype(held_as)


def setup_inputs(seed: int = 0, part: int = 0) -> dict:
    arg_keys = jax.random.split(jax.random.key(seed), 8)
    own_keys = jax.random.split(jax.random.fold_in(arg_keys[7], part), 8)
    return {
        "query_tokens": draw_query_tokens(jax.random.fold_in(jax.random.fold_in(arg_keys[7], part), 71), part),
        "key_tokens": centred(own_keys[1], (KEYS, D), 1.0, 6.0, ((0, 4),)),
        "w_in": centred(arg_keys[2], (D, 3 * HEADS * DH), D ** -0.5, 0.1875),
        "w_out": centred(arg_keys[3], (HEADS * DH, D), (HEADS * DH) ** -0.5, 0.25),
        "out_grad": centred(own_keys[4], (QUERIES, D), 1.0, 6.0, ((0, 16),)),
        "crossing": draw_crossing(jax.random.fold_in(jax.random.fold_in(arg_keys[7], part), 71), part),
        "home": set_ends(jax.random.randint(own_keys[6], (QB,), 0, KB), jax.random.fold_in(own_keys[6], 1), 0, KB - 1).astype(jnp.int32),
    }


NEG = -1e+30

def reference(query_tokens, key_tokens, w_in, w_out, out_grad, crossing, home):
    attn_width = HEADS * DH
    score_scale = 1.0 / math.sqrt(DH)
    query_blocks = QUERIES // BLOCK
    key_blocks = KEYS // BLOCK
    allowed = ((crossing > 0) | (home[:, None] == jnp.arange(key_blocks, dtype=jnp.int32)[None, :])).astype(jnp.float32)
    queries = jnp.dot(query_tokens, w_in[:, :attn_width], preferred_element_type=jnp.float32).astype(jnp.bfloat16)
    projected = jnp.dot(key_tokens, w_in[:, attn_width:], preferred_element_type=jnp.float32).astype(jnp.bfloat16)
    key_heads = projected[:, :attn_width].astype(jnp.float32).reshape(KEYS, HEADS, DH)
    value_heads = projected[:, attn_width:].astype(jnp.float32).reshape(KEYS, HEADS, DH)
    query_heads = queries.astype(jnp.float32).reshape(query_blocks, BLOCK, HEADS, DH)
    element_mask = jnp.repeat(allowed, BLOCK, axis=1)

    def forward_block(operands):
        block_queries, mask_row = operands
        scores = jnp.einsum('qhd,khd->hqk', block_queries, key_heads) * score_scale
        guarded = jnp.where(mask_row[None, None, :] > 0, scores, NEG)
        row_best = lax.optimization_barrier(jnp.max(guarded, axis=2))
        weights = jnp.exp(guarded - row_best[:, :, None]) * mask_row[None, None, :]
        row_total = lax.optimization_barrier(jnp.sum(weights, axis=2))
        rounded = lax.optimization_barrier(weights.astype(jnp.bfloat16)).astype(jnp.float32)
        summed = jnp.einsum('hqk,khd->qhd', rounded, value_heads)
        attended = (summed / row_total.T[:, :, None]).reshape(BLOCK, attn_width).astype(jnp.bfloat16)
        return (attended, row_best + jnp.log(row_total))
    attended, log_total = lax.map(forward_block, (query_heads, element_mask))
    attended = attended.reshape(QUERIES, attn_width)
    output = jnp.dot(attended, w_out, preferred_element_type=jnp.float32).astype(jnp.bfloat16)
    grad_attended = lax.dot_general(out_grad, w_out, (((1,), (1,)), ((), ())), preferred_element_type=jnp.float32).astype(jnp.bfloat16)
    w_out_grad = lax.dot_general(attended, out_grad, (((0,), (0,)), ((), ())), preferred_element_type=jnp.float32)
    spread = lax.optimization_barrier(jnp.sum((grad_attended.astype(jnp.float32) * attended.astype(jnp.float32)).reshape(QUERIES, HEADS, DH), axis=2))
    grad_heads = grad_attended.astype(jnp.float32).reshape(query_blocks, BLOCK, HEADS, DH)
    spread_blocks = spread.reshape(query_blocks, BLOCK, HEADS)

    def backward_block(carried, operands):
        grad_key, grad_value = carried
        block_queries, block_grads, block_log, block_spread, mask_row = operands
        scores = jnp.einsum('qhd,khd->hqk', block_queries, key_heads) * score_scale
        probs = jnp.exp(jnp.where(mask_row[None, None, :] > 0, scores - block_log[:, :, None], NEG))
        grad_probs = jnp.einsum('qhd,khd->hqk', block_grads, value_heads)
        grad_scores = lax.optimization_barrier((probs * (grad_probs - block_spread.T[:, :, None])).astype(jnp.bfloat16)).astype(jnp.float32)
        rounded = lax.optimization_barrier(probs.astype(jnp.bfloat16)).astype(jnp.float32)
        grad_block = jnp.einsum('hqk,khd->qhd', grad_scores, key_heads) * score_scale
        grad_key = grad_key + jnp.einsum('hqk,qhd->khd', grad_scores, block_queries) * score_scale
        grad_value = grad_value + jnp.einsum('hqk,qhd->khd', rounded, block_grads)
        return ((grad_key, grad_value), grad_block.reshape(BLOCK, attn_width).astype(jnp.bfloat16))
    zeros_kv = jnp.zeros((KEYS, HEADS, DH), jnp.float32)
    (grad_key, grad_value), grad_query = lax.scan(backward_block, (zeros_kv, zeros_kv), (query_heads, grad_heads, log_total, spread_blocks, element_mask))
    grad_query = grad_query.reshape(QUERIES, attn_width)
    key_grad_in = jnp.concatenate([grad_key.reshape(KEYS, attn_width), grad_value.reshape(KEYS, attn_width)], axis=1).astype(jnp.bfloat16)
    query_grad = lax.dot_general(grad_query, w_in[:, :attn_width], (((1,), (1,)), ((), ())), preferred_element_type=jnp.float32).astype(jnp.bfloat16)
    key_grad = lax.dot_general(key_grad_in, w_in[:, attn_width:], (((1,), (1,)), ((), ())), preferred_element_type=jnp.float32).astype(jnp.bfloat16)
    query_part = lax.dot_general(query_tokens, grad_query, (((0,), (0,)), ((), ())), preferred_element_type=jnp.float32)
    key_part = lax.dot_general(key_tokens, key_grad_in, (((0,), (0,)), ((), ())), preferred_element_type=jnp.float32)
    w_in_grad = jnp.concatenate([query_part, key_part], axis=1)
    return (output, query_grad, key_grad, w_in_grad, w_out_grad)
```

```python
import functools
import math

import jax
import jax.numpy as jnp
from jax import lax
from jax.experimental import pallas as pl
from jax.experimental.pallas import tpu as pltpu
from jax.sharding import PartitionSpec as P

HEADS = 4
DH = 128
BLOCK = 128
MASK_ROWS = 16
WIDTH = HEADS * DH
F32 = jnp.float32
BF16 = jnp.bfloat16
NT = (((1,), (1,)), ((), ()))
TN = (((0,), (0,)), ((), ()))
NN = (((1,), (0,)), ((), ()))


def mm(a, b, dims):
    return lax.dot_general(a, b, dims, preferred_element_type=F32)


def shape(rows, columns, dtype=BF16):
    return jax.ShapeDtypeStruct((rows, columns), dtype)


VMEM = pl.BlockSpec(memory_space=pltpu.VMEM)
SMEM = pl.BlockSpec(memory_space=pltpu.SMEM)


def columns_of(index, width):
    return pl.ds(pl.multiple_of(index * width, width), width)


def step_from(axis, distance):
    size = lax.axis_size(axis)
    return [((i - distance) % size, i) for i in range(size)]


def sent(block, axis, distance):
    return lax.ppermute(block, axis, step_from(axis, distance))


def call(kernel, out_shape, in_specs, flops, traffic, scratch=(), grid_spec=None, limit=48):
    options = dict(in_specs=in_specs, scratch_shapes=list(scratch)) if grid_spec is None else dict(grid_spec=grid_spec)
    if grid_spec is None:
        options["out_specs"] = jax.tree.map(lambda _: VMEM, out_shape)
    return pl.pallas_call(
        kernel,
        out_shape=out_shape,
        compiler_params=pltpu.CompilerParams(vmem_limit_bytes=limit << 20),
        cost_estimate=pl.CostEstimate(flops=flops, bytes_accessed=traffic, transcendentals=0),
        **options,
    )


def keys_kernel(place, tokens, w_key, w_value, kv):
    kv[:, :DH] = mm(tokens[...], w_key[...], NN).astype(BF16)
    kv[:, DH:] = mm(tokens[...], w_value[...], NN).astype(BF16)


def project_keys(place, key_tokens, w_in):
    rows, width = key_tokens.shape
    return call(
        keys_kernel,
        shape(rows, 2 * DH),
        None,
        4 * rows * width * DH,
        2 * (rows * width + 2 * width * DH + 2 * rows * DH),
        grid_spec=pltpu.PrefetchScalarGridSpec(
            num_scalar_prefetch=1,
            grid=(1,),
            in_specs=[
                pl.BlockSpec((rows, width), lambda i, place: (0, 0)),
                pl.BlockSpec((width, DH), lambda i, place: (0, HEADS + place[0])),
                pl.BlockSpec((width, DH), lambda i, place: (0, 2 * HEADS + place[0])),
            ],
            out_specs=pl.BlockSpec((rows, 2 * DH), lambda i, place: (0, 0)),
        ),
    )(place, key_tokens, w_in, w_in)


def queries_kernel(place, crossing, home, tokens, out_grad, w_in, w_out, *rest):
    outs, (all_q, all_g) = rest[:HEADS], rest[HEADS:]
    all_q[...] = mm(tokens[...], w_in[...], NN).astype(BF16)
    all_g[...] = mm(out_grad[...], w_out[...], NT).astype(BF16)
    lane = lax.broadcasted_iota(jnp.int32, (MASK_ROWS, 2 * DH), 1)
    row = lax.broadcasted_iota(jnp.int32, (MASK_ROWS, 2 * DH), 0)
    mask = jnp.zeros((MASK_ROWS, 2 * DH), F32)
    for j in range(crossing.shape[1]):
        bit = jnp.where((crossing[0, j] > 0) | (home[0] == j), 1.0, 0.0)
        mask = jnp.where((lane == j) & (row == 0), bit, mask)
    for d in range(HEADS):
        head = columns_of(lax.rem(place[0] + d, HEADS), DH)
        outs[d][:BLOCK, :DH] = all_q[:, head]
        outs[d][:BLOCK, DH:] = all_g[:, head]
        outs[d][BLOCK:, :] = mask.astype(BF16)


def project_queries(place, query_tokens, out_grad, w_in, w_out, crossing, home):
    rows, width = query_tokens.shape
    whole = lambda *s: pl.BlockSpec(s, lambda i: (0, 0))
    return pl.pallas_call(
        queries_kernel,
        out_shape=[shape(rows + MASK_ROWS, 2 * DH)] * HEADS,
        grid=(1,),
        in_specs=[
            SMEM,
            SMEM,
            SMEM,
            whole(rows, width),
            whole(rows, width),
            whole(width, WIDTH),
            whole(WIDTH, width),
        ],
        out_specs=[whole(rows + MASK_ROWS, 2 * DH)] * HEADS,
        scratch_shapes=[pltpu.VMEM((rows, WIDTH), BF16)] * 2,
        compiler_params=pltpu.CompilerParams(vmem_limit_bytes=32 << 20),
        cost_estimate=pl.CostEstimate(
            flops=4 * rows * width * WIDTH,
            bytes_accessed=4 * (rows * width + width * WIDTH + rows * WIDTH),
            transcendentals=0,
        ),
    )(place, crossing, home, query_tokens, out_grad, w_in, w_out)


def attention_kernel(place, *refs):
    packs, refs = refs[:HEADS], refs[HEADS:]
    kvs, refs = refs[:HEADS], refs[HEADS:]
    grads, refs = refs[:HEADS], refs[HEADS:]
    backs, (scores, bias, q_all, g_all) = refs[:HEADS], refs[HEADS:]
    chunk = kvs[0].shape[0]
    tiles = chunk // BLOCK
    count = HEADS * BLOCK
    scale = 1.0 / math.sqrt(DH)
    ones = jnp.ones((MASK_ROWS, BLOCK), BF16)
    for d in range(HEADS):
        rows = slice(d * BLOCK, (d + 1) * BLOCK)
        q_all[rows, :] = packs[d][:BLOCK, :DH]
        g_all[rows, :] = packs[d][:BLOCK, DH:]
        allowed = mm(packs[d][BLOCK:, :DH], ones, TN)
        bias[:, rows] = (allowed - 1.0) * 1e30
    q = q_all[...]
    g = g_all[...]
    best = jnp.full((1, count), -3e38, F32)
    for c in range(HEADS):
        soil = lax.rem(place[1] - c + HEADS, HEADS)
        raw = mm(kvs[c][:, :DH], q, NT) * scale
        for j in range(tiles):
            tile = raw[j * BLOCK : (j + 1) * BLOCK, :] + bias[pl.ds(soil * tiles + j, 1), :]
            scores[c * chunk + j * BLOCK : c * chunk + (j + 1) * BLOCK, :] = tile
            best = jnp.maximum(best, jnp.max(tile, axis=0, keepdims=True))
    total = jnp.zeros((1, count), F32)
    summed = jnp.zeros((DH, count), F32)
    for c in range(HEADS):
        part = slice(c * chunk, (c + 1) * chunk)
        weights = jnp.exp(scores[part, :] - best)
        scores[part, :] = weights
        total = total + jnp.sum(weights, axis=0, keepdims=True)
        summed = summed + mm(kvs[c][:, DH:], weights.astype(BF16), TN)
    share = 1.0 / total
    attended = (summed * share).astype(BF16)
    spread = jnp.sum(jnp.transpose(g.astype(F32)) * attended.astype(F32), axis=0, keepdims=True)
    flat = jnp.transpose(attended.astype(F32)).astype(BF16)
    for d in range(HEADS):
        backs[d][:, :DH] = flat[d * BLOCK : (d + 1) * BLOCK, :]
    query_sum = jnp.zeros((DH, count), F32)
    for c in range(HEADS):
        part = slice(c * chunk, (c + 1) * chunk)
        probs = scores[part, :] * share
        grad_probs = mm(kvs[c][:, DH:], g, NT)
        slope = (probs * (grad_probs - spread)).astype(BF16)
        grads[c][:, :DH] = (mm(slope, q, NN) * scale).astype(grads[c].dtype)
        grads[c][:, DH:] = mm(probs.astype(BF16), g, NN).astype(grads[c].dtype)
        query_sum = query_sum + mm(kvs[c][:, :DH], slope, TN)
    flat = (jnp.transpose(query_sum) * scale).astype(BF16)
    for d in range(HEADS):
        backs[d][:, DH:] = flat[d * BLOCK : (d + 1) * BLOCK, :]


def attention(place, packs, kvs):
    chunk = kvs[0].shape[0]
    count = HEADS * BLOCK
    keys = HEADS * chunk
    out = [shape(chunk, 2 * DH, F32)] + [shape(chunk, 2 * DH)] * (HEADS - 1) + [shape(BLOCK, 2 * DH)] * HEADS
    return call(
        attention_kernel,
        out,
        [SMEM] + [VMEM] * (2 * HEADS),
        12 * keys * count * DH,
        8 * keys * 2 * DH,
        scratch=[
            pltpu.VMEM((keys, count), F32),
            pltpu.VMEM((BLOCK, count), F32),
            pltpu.VMEM((count, DH), BF16),
            pltpu.VMEM((count, DH), BF16),
        ],
    )(place, *packs, *kvs)


def query_weights_kernel(place, *refs):
    tokens, refs = refs[:HEADS], refs[HEADS:]
    grads, refs = refs[:HEADS], refs[HEADS:]
    backs, refs = refs[:HEADS], refs[HEADS:]
    outs, (whole,) = refs[:HEADS], refs[HEADS:]
    for half, (left, part) in enumerate(((tokens, slice(DH, 2 * DH)), (grads, slice(0, DH)))):
        term = mm(left[0][...], backs[0][:, part], TN)
        for d in range(1, HEADS):
            term = term + mm(left[d][...], backs[d][:, part], TN)
        whole[:, half * DH : (half + 1) * DH] = term
    rows = whole.shape[0] // HEADS
    for d in range(HEADS):
        outs[d][...] = whole[columns_of(lax.rem(place[1] + d, HEADS), rows), :].astype(outs[d].dtype)


def query_weights(place, tokens, grads, backs):
    width = tokens[0].shape[1]
    rows = width // HEADS
    return call(
        query_weights_kernel,
        [shape(rows, 2 * DH, F32)] + [shape(rows, 2 * DH)] * (HEADS - 1),
        [SMEM] + [VMEM] * (3 * HEADS),
        4 * HEADS * BLOCK * width * DH,
        4 * HEADS * BLOCK * width + 4 * width * DH,
        scratch=[pltpu.VMEM((width, 2 * DH), F32)],
    )(place, *tokens, *grads, *backs)


def sum_kernel(own, *rest):
    total = own[...]
    for other in rest[: HEADS - 1]:
        total = total + other[...].astype(F32)
    outs = rest[HEADS - 1 :]
    width = total.shape[1] // len(outs)
    for i, out in enumerate(outs):
        out[...] = total[:, i * width : (i + 1) * width].astype(BF16)


def sum_parts(parts, pieces):
    rows, width = parts[0].shape
    return call(
        sum_kernel,
        [shape(rows, width // pieces)] * pieces,
        [VMEM] * HEADS,
        rows * width * HEADS,
        12 * rows * width,
    )(*parts)


def key_weights_kernel(place, tokens, own, *rest):
    others, grad, outs, whole = rest[: HEADS - 1], rest[HEADS - 1], rest[HEADS:-1], rest[-1]
    total = own[...]
    for other in others:
        total = total + other[...].astype(F32)
    rounded = total.astype(BF16)
    grad[...] = rounded
    whole[...] = mm(tokens[...], rounded, TN)
    rows = whole.shape[0] // HEADS
    for d in range(HEADS):
        outs[d][...] = whole[columns_of(lax.rem(place[1] + d, HEADS), rows), :].astype(outs[d].dtype)


def key_weights(place, key_tokens, parts):
    count, width = key_tokens.shape
    rows = width // HEADS
    return call(
        key_weights_kernel,
        [shape(count, 2 * DH), shape(rows, 2 * DH, F32)] + [shape(rows, 2 * DH)] * (HEADS - 1),
        [SMEM] + [VMEM] * (HEADS + 1),
        4 * count * width * DH,
        2 * count * width + 10 * count * 2 * DH,
        scratch=[pltpu.VMEM((width, 2 * DH), F32)],
    )(place, key_tokens, *parts)


def query_out_kernel(place, *refs):
    backs, refs = refs[:HEADS], refs[HEADS:]
    w_in, w_out, output, query_grad, att, grad = refs
    for d in range(HEADS):
        head = columns_of(lax.rem(place[0] + d, HEADS), DH)
        att[:, head] = backs[d][:, :DH]
        grad[:, head] = backs[d][:, DH:]
    output[...] = mm(att[...], w_out[...], NN).astype(BF16)
    query_grad[...] = mm(grad[...], w_in[...], NT).astype(BF16)


def query_outputs(place, backs, w_in, w_out):
    width = w_in.shape[0]
    whole = lambda *s: pl.BlockSpec(s, lambda i: (0, 0))
    return pl.pallas_call(
        query_out_kernel,
        out_shape=[shape(BLOCK, width)] * 2,
        grid=(1,),
        in_specs=[SMEM] + [whole(BLOCK, 2 * DH)] * HEADS + [whole(width, WIDTH), whole(WIDTH, width)],
        out_specs=[whole(BLOCK, width)] * 2,
        scratch_shapes=[pltpu.VMEM((BLOCK, WIDTH), BF16)] * 2,
        compiler_params=pltpu.CompilerParams(vmem_limit_bytes=32 << 20),
        cost_estimate=pl.CostEstimate(
            flops=4 * BLOCK * width * WIDTH,
            bytes_accessed=4 * (BLOCK * width + width * WIDTH + BLOCK * WIDTH),
            transcendentals=0,
        ),
    )(place, *backs, w_in, w_out)


def key_out_kernel(place, *refs):
    parts, refs = refs[:HEADS], refs[HEADS:]
    w_key, w_value, out, keys, values = refs
    for d in range(HEADS):
        head = columns_of(lax.rem(place[0] - d + HEADS, HEADS), DH)
        keys[:, head] = parts[d][:, :DH]
        values[:, head] = parts[d][:, DH:]
    out[...] = (mm(keys[...], w_key[...], NT) + mm(values[...], w_value[...], NT)).astype(BF16)


def key_output(place, parts, w_in):
    count = parts[0].shape[0]
    width = w_in.shape[0]
    at = lambda column, *s: pl.BlockSpec(s, lambda i: (0, column))
    return pl.pallas_call(
        key_out_kernel,
        out_shape=shape(count, width),
        grid=(1,),
        in_specs=[SMEM] + [at(0, count, 2 * DH)] * HEADS + [at(1, width, WIDTH), at(2, width, WIDTH)],
        out_specs=at(0, count, width),
        scratch_shapes=[pltpu.VMEM((count, WIDTH), BF16)] * 2,
        compiler_params=pltpu.CompilerParams(vmem_limit_bytes=48 << 20),
        cost_estimate=pl.CostEstimate(
            flops=4 * count * width * WIDTH,
            bytes_accessed=4 * (count * width + width * WIDTH + count * WIDTH),
            transcendentals=0,
        ),
    )(place, *parts, w_in, w_in)


def place_weights_kernel(place, *refs):
    queries, refs = refs[:HEADS], refs[HEADS:]
    keys, refs = refs[:HEADS], refs[HEADS:]
    outs, refs = refs[:HEADS], refs[HEADS:]
    w_in_grad, w_out_grad = refs
    rows = outs[0].shape[0]
    for d in range(HEADS):
        head = lax.rem(place[0] - d + HEADS, HEADS)
        w_in_grad[:, columns_of(head, DH)] = queries[d][...].astype(F32)
        w_in_grad[:, columns_of(HEADS + head, DH)] = keys[d][:, :DH].astype(F32)
        w_in_grad[:, columns_of(2 * HEADS + head, DH)] = keys[d][:, DH:].astype(F32)
        w_out_grad[:, columns_of(head, rows)] = jnp.transpose(outs[d][...].astype(F32))


def place_weights(place, queries, keys, outs):
    rows = queries[0].shape[0]
    return call(
        place_weights_kernel,
        [shape(rows, 3 * WIDTH, F32), shape(DH, HEADS * rows, F32)],
        [SMEM] + [VMEM] * (3 * HEADS),
        rows * 4 * WIDTH,
        6 * rows * 4 * WIDTH,
    )(place, *queries, *keys, *outs)


def head_body(query_tokens, key_tokens, w_in, w_out, out_grad, crossing, home):
    place = jnp.stack([lax.axis_index("stand"), lax.axis_index("soil")]).astype(jnp.int32)
    distances = range(1, HEADS)
    kv = project_keys(place, key_tokens, w_in)
    kvs = [kv] + [sent(kv, "soil", d) for d in distances]
    packs = project_queries(place, query_tokens, out_grad, w_in, w_out, crossing, home)
    packs = [packs[0]] + [sent(packs[d], "stand", d) for d in distances]
    tokens = [query_tokens] + [sent(query_tokens, "stand", d) for d in distances]
    grads = [out_grad] + [sent(out_grad, "stand", d) for d in distances]
    results = attention(place, packs, kvs)
    key_parts, backs = results[:HEADS], results[HEADS:]
    key_parts = [key_parts[0]] + [sent(key_parts[d], "soil", HEADS - d) for d in distances]
    query_parts = query_weights(place, tokens, grads, backs)
    backs = [backs[0]] + [sent(backs[d], "stand", HEADS - d) for d in distances]
    query_parts = [query_parts[0]] + [sent(query_parts[d], "soil", d) for d in distances]
    key_grad_own, *key_weight_parts = key_weights(place, key_tokens, key_parts)
    key_grads = [key_grad_own] + [sent(key_grad_own, "stand", d) for d in distances]
    key_weight_parts = [key_weight_parts[0]] + [sent(key_weight_parts[d], "soil", d) for d in distances]
    output, query_grad = query_outputs(place, backs, w_in, w_out)
    query_weight, out_weight = sum_parts(query_parts, 2)
    (key_weight,) = sum_parts(key_weight_parts, 1)
    query_all = [query_weight] + [sent(query_weight, "stand", d) for d in distances]
    key_all = [key_weight] + [sent(key_weight, "stand", d) for d in distances]
    crosswise = []
    for d in range(HEADS):
        route = [
            (soil * HEADS + stand, stand * HEADS + (soil + d) % HEADS)
            for stand in range(HEADS)
            for soil in range(HEADS)
        ]
        crosswise.append(lax.ppermute(out_weight, ("soil", "stand"), route))
    key_grad = key_output(place, key_grads, w_in)
    w_in_grad, w_out_grad = place_weights(place, query_all, key_all, crosswise)
    return (output, query_grad, key_grad, w_in_grad, w_out_grad)


NEG = -1e30


def from_behind(block, axis, distance):
    devices = range(lax.axis_size(axis))
    route = [((i - distance) % len(devices), i) for i in devices]
    return lax.ppermute(block, axis, route)


def tile_mask(allowed, offset, columns):
    key_blocks = allowed.shape[1]
    column_block = (offset + jnp.arange(columns, dtype=jnp.int32)) // BLOCK
    onehot = (jnp.arange(key_blocks, dtype=jnp.int32)[:, None] == column_block[None, :]).astype(
        jnp.float32
    )
    coarse = jnp.dot(allowed, onehot)
    expanded = jnp.broadcast_to(coarse[:, None, :], (coarse.shape[0], BLOCK, columns))
    return expanded.reshape(coarse.shape[0] * BLOCK, columns)


def guarded_update(update, allowed_mask, operands, carried):
    return update(*operands, allowed_mask, carried)


def forward_tile(queries, key_proj, values, allowed_mask, carried):
    row_best, row_total, summed = carried
    query_count = queries.shape[0]
    key_count = key_proj.shape[0]
    query_heads = queries.reshape(query_count, HEADS, DH)
    key_heads = key_proj.reshape(key_count, HEADS, DH)
    value_heads = values.reshape(key_count, HEADS, DH)
    scores = jnp.einsum(
        "qhd,khd->hqk", query_heads, key_heads, preferred_element_type=jnp.float32
    ) * (1.0 / math.sqrt(DH))
    guarded = jnp.where(allowed_mask[None, :, :] > 0, scores, NEG)
    new_best = jnp.maximum(row_best, jnp.max(guarded, axis=2))
    rescale = jnp.exp(row_best - new_best)
    weights = jnp.exp(guarded - new_best[:, :, None]) * allowed_mask[None, :, :]
    row_total = row_total * rescale + jnp.sum(weights, axis=2)
    contrib = jnp.einsum(
        "hqk,khd->qhd",
        weights.astype(jnp.bfloat16),
        value_heads,
        preferred_element_type=jnp.float32,
    )
    summed = summed.reshape(query_count, HEADS, DH) * rescale.T[:, :, None] + contrib
    return (new_best, row_total, summed.reshape(query_count, HEADS * DH))


def backward_tile(queries, grad_att, log_total, spread, key_proj, values, allowed_mask, carried):
    grad_query, grad_key, grad_value = carried
    query_count = queries.shape[0]
    key_count = key_proj.shape[0]
    query_heads = queries.reshape(query_count, HEADS, DH)
    grad_heads = grad_att.reshape(query_count, HEADS, DH)
    key_heads = key_proj.reshape(key_count, HEADS, DH)
    value_heads = values.reshape(key_count, HEADS, DH)
    score_scale = 1.0 / math.sqrt(DH)
    scores = (
        jnp.einsum("qhd,khd->hqk", query_heads, key_heads, preferred_element_type=jnp.float32)
        * score_scale
    )
    probs = jnp.exp(jnp.where(allowed_mask[None, :, :] > 0, scores - log_total[:, :, None], NEG))
    grad_probs = jnp.einsum(
        "qhd,khd->hqk", grad_heads, value_heads, preferred_element_type=jnp.float32
    )
    grad_scores = (probs * (grad_probs - spread[:, :, None])).astype(jnp.bfloat16)
    query_step = (
        jnp.einsum("hqk,khd->qhd", grad_scores, key_heads, preferred_element_type=jnp.float32)
        * score_scale
    )
    key_step = (
        jnp.einsum("hqk,qhd->khd", grad_scores, query_heads, preferred_element_type=jnp.float32)
        * score_scale
    )
    value_step = jnp.einsum(
        "hqk,qhd->khd", probs.astype(jnp.bfloat16), grad_heads, preferred_element_type=jnp.float32
    )
    grad_query = grad_query + query_step.reshape(query_count, HEADS * DH)
    grad_key = grad_key + key_step.reshape(key_count, HEADS * DH)
    grad_value = grad_value + value_step.reshape(key_count, HEADS * DH)
    return (grad_query, grad_key, grad_value)


def ring_body(query_tokens, key_tokens, w_in, w_out, out_grad, crossing, home):
    attn_width = HEADS * DH
    query_count = query_tokens.shape[0]
    key_count = key_tokens.shape[0]
    soil_count = lax.axis_size("soil")
    soil_index = lax.axis_index("soil")
    stand_count = lax.axis_size("stand")
    stand_index = lax.axis_index("stand")
    total_blocks = key_count * soil_count // BLOCK
    allowed = (
        (crossing > 0) | (home[:, None] == jnp.arange(total_blocks, dtype=jnp.int32)[None, :])
    ).astype(jnp.float32)
    queries = jnp.dot(
        query_tokens, w_in[:, :attn_width], preferred_element_type=jnp.float32
    ).astype(jnp.bfloat16)
    projected = jnp.dot(
        key_tokens, w_in[:, attn_width:], preferred_element_type=jnp.float32
    ).astype(jnp.bfloat16)
    key_proj = projected[:, :attn_width]
    values = projected[:, attn_width:]
    key_offset = soil_index * key_count
    start_state = (
        jnp.full((HEADS, query_count), NEG, jnp.float32),
        jnp.zeros((HEADS, query_count), jnp.float32),
        jnp.zeros((query_count, attn_width), jnp.float32),
    )

    def forward_turn(turn_index, carried):
        moving, running = carried
        allowed_mask = tile_mask(moving[1].astype(jnp.float32), key_offset, key_count)
        running = guarded_update(forward_tile, allowed_mask, (moving[0], key_proj, values), running)
        moving = from_behind((moving[0], moving[1]), "soil", 1)
        running = from_behind(running, "soil", 1)
        return (moving, running)

    moving, running = lax.fori_loop(
        0, soil_count, forward_turn, ((queries, allowed.astype(jnp.bfloat16)), start_state)
    )
    row_best, row_total, summed = running
    attended = (
        (summed.reshape(query_count, HEADS, DH) / row_total.T[:, :, None])
        .reshape(query_count, attn_width)
        .astype(jnp.bfloat16)
    )
    log_total = row_best + jnp.log(row_total)
    output = jnp.dot(attended, w_out, preferred_element_type=jnp.float32).astype(jnp.bfloat16)
    grad_attended = lax.dot_general(
        out_grad, w_out, (((1,), (1,)), ((), ())), preferred_element_type=jnp.float32
    ).astype(jnp.bfloat16)
    spread = jnp.sum(
        (grad_attended.astype(jnp.float32) * attended.astype(jnp.float32)).reshape(
            query_count, HEADS, DH
        ),
        axis=2,
    ).T
    zero_query = jnp.zeros((query_count, attn_width), jnp.float32)
    zero_key = jnp.zeros((key_count, attn_width), jnp.float32)

    def backward_turn(turn_index, carried):
        moving, query_stats, grad_key, grad_value = carried
        allowed_mask = tile_mask(moving[2].astype(jnp.float32), key_offset, key_count)
        grad_query, grad_key, grad_value = guarded_update(
            backward_tile,
            allowed_mask,
            (moving[0], moving[1], query_stats[0], query_stats[1], key_proj, values),
            (query_stats[2], grad_key, grad_value),
        )
        moving = from_behind((moving[0], moving[1], moving[2]), "soil", 1)
        query_stats = from_behind((query_stats[0], query_stats[1], grad_query), "soil", 1)
        return (moving, query_stats, grad_key, grad_value)

    moving, query_stats, grad_key, grad_value = lax.fori_loop(
        0,
        soil_count,
        backward_turn,
        (
            (queries, grad_attended, allowed.astype(jnp.bfloat16)),
            (log_total, spread, zero_query),
            zero_key,
            zero_key,
        ),
    )
    grad_query = query_stats[2]
    grad_key, grad_value = lax.psum((grad_key, grad_value), "stand")
    key_grad_in = jnp.concatenate([grad_key, grad_value], axis=1).astype(jnp.bfloat16)
    query_grad_in = grad_query.astype(jnp.bfloat16)
    query_grad = lax.dot_general(
        query_grad_in,
        w_in[:, :attn_width],
        (((1,), (1,)), ((), ())),
        preferred_element_type=jnp.float32,
    ).astype(jnp.bfloat16)
    key_grad = lax.dot_general(
        key_grad_in,
        w_in[:, attn_width:],
        (((1,), (1,)), ((), ())),
        preferred_element_type=jnp.float32,
    ).astype(jnp.bfloat16)
    stand_rows = key_count // stand_count
    key_slice = lax.dynamic_slice_in_dim(key_tokens, stand_index * stand_rows, stand_rows, 0)
    grad_slice = lax.dynamic_slice_in_dim(key_grad_in, stand_index * stand_rows, stand_rows, 0)
    query_part = lax.dot_general(
        query_tokens, query_grad_in, (((0,), (0,)), ((), ())), preferred_element_type=jnp.float32
    )
    key_part = lax.dot_general(
        key_slice, grad_slice, (((0,), (0,)), ((), ())), preferred_element_type=jnp.float32
    )
    w_in_part = lax.psum_scatter(
        jnp.concatenate([query_part, key_part], axis=1), "soil", scatter_dimension=0, tiled=True
    )
    w_out_part = lax.psum_scatter(
        lax.dot_general(
            attended, out_grad, (((0,), (0,)), ((), ())), preferred_element_type=jnp.float32
        ),
        "soil",
        scatter_dimension=0,
        tiled=True,
    )
    w_in_grad, w_out_grad = lax.psum((w_in_part, w_out_part), "stand")
    return (output, query_grad, key_grad, w_in_grad, w_out_grad)


def solution(mesh):
    in_specs = (
        P(("field", "stand", "soil"), None),
        P(("field", "soil"), None),
        P(),
        P(),
        P(("field", "stand", "soil"), None),
        P(("field", "stand", "soil"), None),
        P(("field", "stand", "soil")),
    )
    out_specs = (
        P(("field", "stand", "soil"), None),
        P(("field", "stand", "soil"), None),
        P(("field", "soil"), None),
        P(("field", "soil"), None),
        P(("field", "soil"), None),
    )
    square = mesh.shape["stand"] == HEADS and mesh.shape["soil"] == HEADS
    body = head_body if square else ring_body
    return jax.shard_map(body, mesh=mesh, in_specs=in_specs, out_specs=out_specs, check_vma=False)
```

```python
import math

import jax
import jax.numpy as jnp
from jax import lax
from jax.experimental import pallas as pl
from jax.experimental.pallas import tpu as pltpu
from jax.sharding import PartitionSpec as P

HEADS = 4
DH = 128
BLOCK = 128
MASK_ROWS = 16
PACK = BLOCK + MASK_ROWS
LIMIT = 60
WIDTH = HEADS * DH
F32 = jnp.float32
BF16 = jnp.bfloat16
NT = (((1,), (1,)), ((), ()))
TN = (((0,), (0,)), ((), ()))
NN = (((1,), (0,)), ((), ()))


def mm(a, b, dims):
    return lax.dot_general(a, b, dims, preferred_element_type=F32)


def shape(rows, columns, dtype=BF16):
    return jax.ShapeDtypeStruct((rows, columns), dtype)


SMEM = pl.BlockSpec(memory_space=pltpu.SMEM)


def columns_of(index, width):
    return pl.ds(pl.multiple_of(index * width, width), width)


def step_from(axis, distance):
    size = lax.axis_size(axis)
    return [((i - distance) % size, i) for i in range(size)]


def sent(block, axis, distance):
    return lax.ppermute(block, axis, step_from(axis, distance))


def whole(block):
    return pl.BlockSpec(block.shape, lambda *_: (0,) * len(block.shape))


def call(kernel, out_shape, operands, flops, scratch=(), in_specs=None):
    if in_specs is None:
        in_specs = [SMEM if x.dtype == jnp.int32 else whole(x) for x in operands]
    outs = jax.tree.leaves(out_shape)
    traffic = sum(2 * math.prod(x.shape) for x in (*operands, *outs))
    return pl.pallas_call(
        kernel,
        out_shape=out_shape,
        grid=(1,),
        in_specs=in_specs,
        out_specs=jax.tree.map(whole, out_shape),
        scratch_shapes=list(scratch),
        compiler_params=pltpu.CompilerParams(vmem_limit_bytes=LIMIT << 20),
        cost_estimate=pl.CostEstimate(flops=flops, bytes_accessed=traffic, transcendentals=0),
    )(*operands)


def keys_kernel(place, tokens, w_key, w_value, *refs):
    outs, (keys, values) = refs[:HEADS], refs[HEADS:]
    keys[...] = mm(tokens[...], w_key[...], NN).astype(BF16)
    values[...] = mm(tokens[...], w_value[...], NN).astype(BF16)
    for d in range(HEADS):
        head = columns_of(lax.rem(place[1] + d, HEADS), DH)
        outs[d][:, :DH] = keys[:, head]
        outs[d][:, DH:] = values[:, head]


def third(w_in, index):
    return pl.BlockSpec((w_in.shape[0], WIDTH), lambda i: (0, index))


def project_keys(place, key_tokens, w_in):
    rows, width = key_tokens.shape
    return call(
        keys_kernel,
        [shape(rows, 2 * DH)] * HEADS,
        (place, key_tokens, w_in, w_in),
        4 * rows * width * WIDTH,
        scratch=[pltpu.VMEM((rows, WIDTH), BF16)] * 2,
        in_specs=[SMEM, whole(key_tokens), third(w_in, 1), third(w_in, 2)],
    )


def queries_kernel(place, crossing, home, tokens, grad, w_in, w_out, packs, *slices):
    lane = lax.broadcasted_iota(jnp.int32, (MASK_ROWS, 2 * DH), 1)
    row = lax.broadcasted_iota(jnp.int32, (MASK_ROWS, 2 * DH), 0)
    mask = jnp.zeros((MASK_ROWS, 2 * DH), F32)
    for j in range(crossing.shape[1]):
        bit = jnp.where((crossing[0, j] > 0) | (home[0] == j), 1.0, 0.0)
        mask = jnp.where((lane == j) & (row == 0), bit, mask)
    for half, product in enumerate((mm(tokens[...], w_in[...], NN), mm(grad[...], w_out[...], NT))):
        product = product.astype(BF16)
        for h in range(HEADS):
            packs[h * PACK : h * PACK + BLOCK, half * DH : (half + 1) * DH] = product[:, h * DH : (h + 1) * DH]
    part = tokens.shape[1] // HEADS
    for d in range(HEADS):
        packs[d * PACK + BLOCK : (d + 1) * PACK, :] = mask.astype(BF16)
        columns = columns_of(lax.rem(place[0] + d, HEADS), part)
        slices[d][:, :part] = tokens[:, columns]
        slices[d][:, part:] = grad[:, columns]


def project_queries(place, query_tokens, out_grad, w_in, w_out, crossing, home):
    rows, width = query_tokens.shape
    return call(
        queries_kernel,
        [shape(HEADS * PACK, 2 * DH)] + [shape(rows, 2 * width // HEADS)] * HEADS,
        (place, crossing, home, query_tokens, out_grad, w_in, w_out),
        4 * rows * width * WIDTH,
        in_specs=[SMEM] * 3 + [whole(query_tokens), whole(out_grad), third(w_in, 0), whole(w_out)],
    )


def side_kernel(place, key_tokens, *refs):
    slices, side = refs[:HEADS], refs[HEADS]
    rows, width = slices[0].shape
    for d in range(HEADS):
        side[d * rows : (d + 1) * rows, :width] = slices[d][...]
    part = width // 2
    side[:, width:] = key_tokens[:, columns_of(place[0], part)]


def joined(place, key_tokens, slices):
    width = 3 * key_tokens.shape[1] // HEADS
    return call(side_kernel, shape(key_tokens.shape[0], width), (place, key_tokens, *slices), 0)


def attend(place, packs, kvs, back, scores, bias, q_all, g_all, emit):
    chunk = kvs[0].shape[0]
    tiles = chunk // BLOCK
    count = HEADS * BLOCK
    scale = 1.0 / math.sqrt(DH)
    ones = jnp.ones((MASK_ROWS, BLOCK), BF16)
    for d in range(HEADS):
        rows = slice(d * BLOCK, (d + 1) * BLOCK)
        q_all[rows, :] = packs[d * PACK : d * PACK + BLOCK, :DH]
        g_all[rows, :] = packs[d * PACK : d * PACK + BLOCK, DH:]
        allowed = mm(packs[d * PACK + BLOCK : (d + 1) * PACK, :DH], ones, TN)
        bias[:, rows] = (allowed - 1.0) * 1e30
    q = q_all[...]
    g = g_all[...]
    best = jnp.full((1, count), -3e38, F32)
    for c in range(HEADS):
        first = lax.rem(place[1] - c + HEADS, HEADS) * tiles
        raw = mm(kvs[c][:, :DH], q, NT) * scale
        for j in range(tiles):
            tile = raw[j * BLOCK : (j + 1) * BLOCK, :] + bias[pl.ds(first + j, 1), :]
            scores[c * chunk + j * BLOCK : c * chunk + (j + 1) * BLOCK, :] = tile
            best = jnp.maximum(best, jnp.max(tile, axis=0, keepdims=True))
    total = jnp.zeros((1, count), F32)
    summed = jnp.zeros((DH, count), F32)
    for c in range(HEADS):
        part = slice(c * chunk, (c + 1) * chunk)
        weights = jnp.exp(scores[part, :] - best)
        scores[part, :] = weights
        total = total + jnp.sum(weights, axis=0, keepdims=True)
        summed = summed + mm(kvs[c][:, DH:], weights.astype(BF16), TN)
    share = 1.0 / total
    attended = (summed * share).astype(BF16)
    spread = jnp.sum(jnp.transpose(g.astype(F32)) * attended.astype(F32), axis=0, keepdims=True)
    back[:, :DH] = jnp.transpose(attended.astype(F32)).astype(BF16)
    query_sum = jnp.zeros((DH, count), F32)
    for c in range(HEADS):
        part = slice(c * chunk, (c + 1) * chunk)
        probs = scores[part, :] * share
        grad_probs = mm(kvs[c][:, DH:], g, NT)
        slope = (probs * (grad_probs - spread)).astype(BF16)
        emit(c, mm(slope, q, NN), mm(probs.astype(BF16), g, NN))
        query_sum = query_sum + mm(kvs[c][:, :DH], slope, TN)
    back[:, DH:] = (jnp.transpose(query_sum) * scale).astype(BF16)


def first_kernel(place, packs, *refs):
    kvs, (back, total, *scratch) = refs[:HEADS], refs[HEADS:]
    chunk = kvs[0].shape[0]

    def emit(c, key_step, value_step):
        total[c * chunk : (c + 1) * chunk, :DH] = key_step
        total[c * chunk : (c + 1) * chunk, DH:] = value_step

    attend(place, packs, kvs, back, *scratch, emit)


def middle_kernel(place, packs, *refs):
    kvs, (before, back, total, *scratch) = refs[:HEADS], refs[HEADS:]
    chunk = kvs[0].shape[0]

    def emit(c, key_step, value_step):
        rows = slice(c * chunk, (c + 1) * chunk)
        total[rows, :DH] = before[rows, :DH] + key_step
        total[rows, DH:] = before[rows, DH:] + value_step

    attend(place, packs, kvs, back, *scratch, emit)


def last_kernel(place, packs, *refs):
    kvs, (before, other, own_back, back, home_parts, *scratch) = refs[:HEADS], refs[HEADS:]
    chunk = kvs[0].shape[0]
    scale = 1.0 / math.sqrt(DH)

    def emit(c, key_step, value_step):
        rows = slice(c * chunk, (c + 1) * chunk)
        start = lax.rem(place[1] - c + HEADS, HEADS) * (chunk + BLOCK)
        out = pl.ds(pl.multiple_of(start, BLOCK), chunk)
        key_sum = (before[rows, :DH] + key_step) + other[rows, :DH]
        home_parts[out, :DH] = (key_sum * scale).astype(BF16)
        home_parts[out, DH:] = ((before[rows, DH:] + value_step) + other[rows, DH:]).astype(BF16)

    attend(place, packs, kvs, back, *scratch, emit)
    for h in range(HEADS):
        start = h * (chunk + BLOCK) + chunk
        home_parts[start : start + BLOCK, :] = own_back[h * BLOCK : (h + 1) * BLOCK, :]


def attention(kernel, place, packs, kvs, extra):
    chunk = kvs[0].shape[0]
    keys = HEADS * chunk
    count = HEADS * BLOCK
    last = shape(HEADS * (chunk + BLOCK), 2 * DH) if len(extra) == 3 else shape(keys, 2 * DH, F32)
    return call(
        kernel,
        [shape(count, 2 * DH), last],
        (place, packs, *kvs, *extra),
        12 * keys * count * DH,
        scratch=[
            pltpu.VMEM((keys, count), F32),
            pltpu.VMEM((BLOCK, count), F32),
            pltpu.VMEM((count, DH), BF16),
            pltpu.VMEM((count, DH), BF16),
        ],
    )


def weights_kernel(place, home_parts, *refs):
    backs, refs = refs[:HEADS], refs[HEADS:]
    sides, (inner, outer) = refs[:HEADS], refs[HEADS:]
    part = inner.shape[0]
    chunk = sides[0].shape[0]
    for_keys, for_queries, for_output = 0.0, 0.0, 0.0
    for e in range(HEADS):
        soil = lax.rem(place[1] - e + HEADS, HEADS)
        rows = pl.ds(pl.multiple_of(soil * (chunk + BLOCK), BLOCK), chunk)
        for_keys = for_keys + mm(sides[e][:, 2 * part :], home_parts[rows, :], TN)
        block = columns_of(soil, BLOCK)
        right = jnp.concatenate([backs[d][block, :] for d in range(HEADS)], axis=0)
        for_queries = for_queries + mm(sides[e][:, :part], right[:, DH:], TN)
        for_output = for_output + mm(sides[e][:, part : 2 * part], right[:, :DH], TN)
    inner[:, : 2 * DH] = for_keys.astype(BF16)
    inner[:, 2 * DH :] = for_queries.astype(BF16)
    outer[...] = for_output.astype(BF16)


def weights_of(place, home_parts, backs, sides):
    part = sides[0].shape[1] // 3
    return call(
        weights_kernel,
        [shape(part, 3 * DH), shape(part, DH)],
        (place, home_parts, *backs, *sides),
        8 * HEADS * sides[0].shape[0] * part * DH,
    )


def home_kernel(parts, w_query, w_key, w_value, w_out, key_grad, output, query_grad):
    count = key_grad.shape[0]
    chunks = [parts.at[h * (count + BLOCK) : (h + 1) * (count + BLOCK), :] for h in range(HEADS)]
    keys = jnp.concatenate([x[:count, :DH] for x in chunks], axis=1)
    values = jnp.concatenate([x[:count, DH:] for x in chunks], axis=1)
    key_grad[...] = (mm(keys, w_key[...], NT) + mm(values, w_value[...], NT)).astype(BF16)
    attended = jnp.concatenate([x[count:, :DH] for x in chunks], axis=1)
    output[...] = mm(attended, w_out[...], NN).astype(BF16)
    grad = jnp.concatenate([x[count:, DH:] for x in chunks], axis=1)
    query_grad[...] = mm(grad, w_query[...], NT).astype(BF16)


def home_outputs(parts, w_in, w_out):
    width = w_in.shape[0]
    count = parts.shape[0] // HEADS - BLOCK
    return call(
        home_kernel,
        [shape(count, width), shape(BLOCK, width), shape(BLOCK, width)],
        (parts, w_in, w_in, w_in, w_out),
        4 * (count + BLOCK) * width * WIDTH,
        in_specs=[whole(parts), third(w_in, 0), third(w_in, 1), third(w_in, 2), whole(w_out)],
    )


def place_weights_kernel(place, *refs):
    inner, outer, (w_in_grad, w_out_grad) = refs[:HEADS], refs[HEADS : 2 * HEADS], refs[2 * HEADS :]
    rows = inner[0].shape[0]
    for d in range(HEADS):
        index = lax.rem(place[0] - d + HEADS, HEADS)
        w_in_grad[:, columns_of(index, DH)] = inner[d][:, 2 * DH :].astype(F32)
        w_in_grad[:, columns_of(HEADS + index, DH)] = inner[d][:, :DH].astype(F32)
        w_in_grad[:, columns_of(2 * HEADS + index, DH)] = inner[d][:, DH : 2 * DH].astype(F32)
        w_out_grad[:, columns_of(index, rows)] = jnp.transpose(outer[d][...].astype(F32))


def place_weights(place, inner, outer):
    rows = inner[0].shape[0]
    return call(
        place_weights_kernel,
        [shape(rows, 3 * WIDTH, F32), shape(DH, HEADS * rows, F32)],
        (place, *inner, *outer),
        rows * 4 * WIDTH,
    )


def after(value, *others):
    return lax.optimization_barrier((value, *others))[0]


def swapped(block, axis):
    return lax.all_to_all(block, axis, 0, 0, tiled=True)


def spread_to(block, axis):
    return [block] + [sent(block, axis, d) for d in range(1, HEADS)]


def head_body(query_tokens, key_tokens, w_in, w_out, out_grad, crossing, home):
    place = jnp.stack([lax.axis_index("stand"), lax.axis_index("soil")]).astype(jnp.int32)
    distances = range(1, HEADS)
    packs, *slices = project_queries(place, query_tokens, out_grad, w_in, w_out, crossing, home)
    packs = swapped(packs, "soil")
    kvs = project_keys(place, key_tokens, w_in)
    kvs = [kvs[0]] + [sent(kvs[d], "soil", d) for d in distances]
    slices = [slices[0]] + [sent(slices[d], "stand", d) for d in distances]
    planes = spread_to(packs, "stand")
    sides = spread_to(joined(place, key_tokens, slices), "soil")
    back_0, even = attention(first_kernel, place, planes[0], kvs, ())
    back_1, odd = attention(first_kernel, place, planes[1], kvs, ())
    back_3, odd = attention(middle_kernel, place, planes[3], kvs, (odd,))
    back_2, home_parts = attention(last_kernel, place, planes[2], kvs, (even, odd, back_0))
    inner, outer = weights_of(place, home_parts, [back_0, back_1, back_2, back_3], sides)
    home_parts = swapped(home_parts, "soil")
    key_grad, output, query_grad = home_outputs(home_parts, w_in, w_out)
    outer = spread_to(outer, "stand")
    crosswise = []
    for d in range(HEADS):
        route = [
            (soil * HEADS + stand, stand * HEADS + (soil + d) % HEADS)
            for stand in range(HEADS)
            for soil in range(HEADS)
        ]
        crosswise.append(lax.ppermute(inner, ("soil", "stand"), route))
    w_in_grad, w_out_grad = place_weights(place, crosswise, outer)
    return (output, query_grad, key_grad, w_in_grad, w_out_grad)


NEG = -1e30


def from_behind(block, axis, distance):
    devices = range(lax.axis_size(axis))
    route = [((i - distance) % len(devices), i) for i in devices]
    return lax.ppermute(block, axis, route)


def tile_mask(allowed, offset, columns):
    key_blocks = allowed.shape[1]
    column_block = (offset + jnp.arange(columns, dtype=jnp.int32)) // BLOCK
    onehot = (jnp.arange(key_blocks, dtype=jnp.int32)[:, None] == column_block[None, :]).astype(
        jnp.float32
    )
    coarse = jnp.dot(allowed, onehot)
    expanded = jnp.broadcast_to(coarse[:, None, :], (coarse.shape[0], BLOCK, columns))
    return expanded.reshape(coarse.shape[0] * BLOCK, columns)


def guarded_update(update, allowed_mask, operands, carried):
    return update(*operands, allowed_mask, carried)


def forward_tile(queries, key_proj, values, allowed_mask, carried):
    row_best, row_total, summed = carried
    query_count = queries.shape[0]
    key_count = key_proj.shape[0]
    query_heads = queries.reshape(query_count, HEADS, DH)
    key_heads = key_proj.reshape(key_count, HEADS, DH)
    value_heads = values.reshape(key_count, HEADS, DH)
    scores = jnp.einsum(
        "qhd,khd->hqk", query_heads, key_heads, preferred_element_type=jnp.float32
    ) * (1.0 / math.sqrt(DH))
    guarded = jnp.where(allowed_mask[None, :, :] > 0, scores, NEG)
    new_best = jnp.maximum(row_best, jnp.max(guarded, axis=2))
    rescale = jnp.exp(row_best - new_best)
    weights = jnp.exp(guarded - new_best[:, :, None]) * allowed_mask[None, :, :]
    row_total = row_total * rescale + jnp.sum(weights, axis=2)
    contrib = jnp.einsum(
        "hqk,khd->qhd",
        weights.astype(jnp.bfloat16),
        value_heads,
        preferred_element_type=jnp.float32,
    )
    summed = summed.reshape(query_count, HEADS, DH) * rescale.T[:, :, None] + contrib
    return (new_best, row_total, summed.reshape(query_count, HEADS * DH))


def backward_tile(queries, grad_att, log_total, spread, key_proj, values, allowed_mask, carried):
    grad_query, grad_key, grad_value = carried
    query_count = queries.shape[0]
    key_count = key_proj.shape[0]
    query_heads = queries.reshape(query_count, HEADS, DH)
    grad_heads = grad_att.reshape(query_count, HEADS, DH)
    key_heads = key_proj.reshape(key_count, HEADS, DH)
    value_heads = values.reshape(key_count, HEADS, DH)
    score_scale = 1.0 / math.sqrt(DH)
    scores = (
        jnp.einsum("qhd,khd->hqk", query_heads, key_heads, preferred_element_type=jnp.float32)
        * score_scale
    )
    probs = jnp.exp(jnp.where(allowed_mask[None, :, :] > 0, scores - log_total[:, :, None], NEG))
    grad_probs = jnp.einsum(
        "qhd,khd->hqk", grad_heads, value_heads, preferred_element_type=jnp.float32
    )
    grad_scores = (probs * (grad_probs - spread[:, :, None])).astype(jnp.bfloat16)
    query_step = (
        jnp.einsum("hqk,khd->qhd", grad_scores, key_heads, preferred_element_type=jnp.float32)
        * score_scale
    )
    key_step = (
        jnp.einsum("hqk,qhd->khd", grad_scores, query_heads, preferred_element_type=jnp.float32)
        * score_scale
    )
    value_step = jnp.einsum(
        "hqk,qhd->khd", probs.astype(jnp.bfloat16), grad_heads, preferred_element_type=jnp.float32
    )
    grad_query = grad_query + query_step.reshape(query_count, HEADS * DH)
    grad_key = grad_key + key_step.reshape(key_count, HEADS * DH)
    grad_value = grad_value + value_step.reshape(key_count, HEADS * DH)
    return (grad_query, grad_key, grad_value)


def ring_body(query_tokens, key_tokens, w_in, w_out, out_grad, crossing, home):
    attn_width = HEADS * DH
    query_count = query_tokens.shape[0]
    key_count = key_tokens.shape[0]
    soil_count = lax.axis_size("soil")
    soil_index = lax.axis_index("soil")
    stand_count = lax.axis_size("stand")
    stand_index = lax.axis_index("stand")
    total_blocks = key_count * soil_count // BLOCK
    allowed = (
        (crossing > 0) | (home[:, None] == jnp.arange(total_blocks, dtype=jnp.int32)[None, :])
    ).astype(jnp.float32)
    queries = jnp.dot(
        query_tokens, w_in[:, :attn_width], preferred_element_type=jnp.float32
    ).astype(jnp.bfloat16)
    projected = jnp.dot(
        key_tokens, w_in[:, attn_width:], preferred_element_type=jnp.float32
    ).astype(jnp.bfloat16)
    key_proj = projected[:, :attn_width]
    values = projected[:, attn_width:]
    key_offset = soil_index * key_count
    start_state = (
        jnp.full((HEADS, query_count), NEG, jnp.float32),
        jnp.zeros((HEADS, query_count), jnp.float32),
        jnp.zeros((query_count, attn_width), jnp.float32),
    )

    def forward_turn(turn_index, carried):
        moving, running = carried
        allowed_mask = tile_mask(moving[1].astype(jnp.float32), key_offset, key_count)
        running = guarded_update(forward_tile, allowed_mask, (moving[0], key_proj, values), running)
        moving = from_behind((moving[0], moving[1]), "soil", 1)
        running = from_behind(running, "soil", 1)
        return (moving, running)

    moving, running = lax.fori_loop(
        0, soil_count, forward_turn, ((queries, allowed.astype(jnp.bfloat16)), start_state)
    )
    row_best, row_total, summed = running
    attended = (
        (summed.reshape(query_count, HEADS, DH) / row_total.T[:, :, None])
        .reshape(query_count, attn_width)
        .astype(jnp.bfloat16)
    )
    log_total = row_best + jnp.log(row_total)
    output = jnp.dot(attended, w_out, preferred_element_type=jnp.float32).astype(jnp.bfloat16)
    grad_attended = lax.dot_general(
        out_grad, w_out, (((1,), (1,)), ((), ())), preferred_element_type=jnp.float32
    ).astype(jnp.bfloat16)
    spread = jnp.sum(
        (grad_attended.astype(jnp.float32) * attended.astype(jnp.float32)).reshape(
            query_count, HEADS, DH
        ),
        axis=2,
    ).T
    zero_query = jnp.zeros((query_count, attn_width), jnp.float32)
    zero_key = jnp.zeros((key_count, attn_width), jnp.float32)

    def backward_turn(turn_index, carried):
        moving, query_stats, grad_key, grad_value = carried
        allowed_mask = tile_mask(moving[2].astype(jnp.float32), key_offset, key_count)
        grad_query, grad_key, grad_value = guarded_update(
            backward_tile,
            allowed_mask,
            (moving[0], moving[1], query_stats[0], query_stats[1], key_proj, values),
            (query_stats[2], grad_key, grad_value),
        )
        moving = from_behind((moving[0], moving[1], moving[2]), "soil", 1)
        query_stats = from_behind((query_stats[0], query_stats[1], grad_query), "soil", 1)
        return (moving, query_stats, grad_key, grad_value)

    moving, query_stats, grad_key, grad_value = lax.fori_loop(
        0,
        soil_count,
        backward_turn,
        (
            (queries, grad_attended, allowed.astype(jnp.bfloat16)),
            (log_total, spread, zero_query),
            zero_key,
            zero_key,
        ),
    )
    grad_query = query_stats[2]
    grad_key, grad_value = lax.psum((grad_key, grad_value), "stand")
    key_grad_in = jnp.concatenate([grad_key, grad_value], axis=1).astype(jnp.bfloat16)
    query_grad_in = grad_query.astype(jnp.bfloat16)
    query_grad = lax.dot_general(
        query_grad_in,
        w_in[:, :attn_width],
        (((1,), (1,)), ((), ())),
        preferred_element_type=jnp.float32,
    ).astype(jnp.bfloat16)
    key_grad = lax.dot_general(
        key_grad_in,
        w_in[:, attn_width:],
        (((1,), (1,)), ((), ())),
        preferred_element_type=jnp.float32,
    ).astype(jnp.bfloat16)
    stand_rows = key_count // stand_count
    key_slice = lax.dynamic_slice_in_dim(key_tokens, stand_index * stand_rows, stand_rows, 0)
    grad_slice = lax.dynamic_slice_in_dim(key_grad_in, stand_index * stand_rows, stand_rows, 0)
    query_part = lax.dot_general(
        query_tokens, query_grad_in, (((0,), (0,)), ((), ())), preferred_element_type=jnp.float32
    )
    key_part = lax.dot_general(
        key_slice, grad_slice, (((0,), (0,)), ((), ())), preferred_element_type=jnp.float32
    )
    w_in_part = lax.psum_scatter(
        jnp.concatenate([query_part, key_part], axis=1), "soil", scatter_dimension=0, tiled=True
    )
    w_out_part = lax.psum_scatter(
        lax.dot_general(
            attended, out_grad, (((0,), (0,)), ((), ())), preferred_element_type=jnp.float32
        ),
        "soil",
        scatter_dimension=0,
        tiled=True,
    )
    w_in_grad, w_out_grad = lax.psum((w_in_part, w_out_part), "stand")
    return (output, query_grad, key_grad, w_in_grad, w_out_grad)


def solution(mesh):
    in_specs = (
        P(("field", "stand", "soil"), None),
        P(("field", "soil"), None),
        P(),
        P(),
        P(("field", "stand", "soil"), None),
        P(("field", "stand", "soil"), None),
        P(("field", "stand", "soil")),
    )
    out_specs = (
        P(("field", "stand", "soil"), None),
        P(("field", "stand", "soil"), None),
        P(("field", "soil"), None),
        P(("field", "soil"), None),
        P(("field", "soil"), None),
    )
    square = mesh.shape["stand"] == HEADS and mesh.shape["soil"] == HEADS
    body = head_body if square else ring_body
    return jax.shard_map(body, mesh=mesh, in_specs=in_specs, out_specs=out_specs, check_vma=False)
```

```python
import functools
import math

import jax
import jax.numpy as jnp
from jax import lax
from jax.experimental import pallas as pl
from jax.experimental.pallas import tpu as pltpu
from jax.sharding import PartitionSpec as P

HEADS = 4
DH = 128
BLOCK = 128
MASK_ROWS = 16
PACK = BLOCK + MASK_ROWS
LIMIT = 60
WIDTH = HEADS * DH
F32 = jnp.float32
BF16 = jnp.bfloat16
NT = (((1,), (1,)), ((), ()))
TN = (((0,), (0,)), ((), ()))
NN = (((1,), (0,)), ((), ()))


def mm(a, b, dims):
    return lax.dot_general(a, b, dims, preferred_element_type=F32)


def shape(rows, columns, dtype=BF16):
    return jax.ShapeDtypeStruct((rows, columns), dtype)


SMEM = pl.BlockSpec(memory_space=pltpu.SMEM)
ANY = pl.BlockSpec(memory_space=pl.ANY)


def columns_of(index, width):
    return pl.ds(pl.multiple_of(index * width, width), width)


def step_from(axis, distance):
    size = lax.axis_size(axis)
    return [((i - distance) % size, i) for i in range(size)]


def sent(block, axis, distance):
    return lax.ppermute(block, axis, step_from(axis, distance))


def whole(block):
    return pl.BlockSpec(block.shape, lambda *_: (0,) * len(block.shape))


def call(kernel, out_shape, operands, flops, scratch=(), in_specs=None, out_specs=None):
    if in_specs is None:
        in_specs = [SMEM if x.dtype == jnp.int32 else whole(x) for x in operands]
    outs = jax.tree.leaves(out_shape)
    traffic = sum(2 * math.prod(x.shape) for x in (*operands, *outs))
    return pl.pallas_call(
        kernel,
        out_shape=out_shape,
        grid=(1,),
        in_specs=in_specs,
        out_specs=jax.tree.map(whole, out_shape) if out_specs is None else out_specs,
        scratch_shapes=list(scratch),
        compiler_params=pltpu.CompilerParams(vmem_limit_bytes=LIMIT << 20),
        cost_estimate=pl.CostEstimate(flops=flops, bytes_accessed=traffic, transcendentals=0),
    )(*operands)


def third(w_in, index):
    return pl.BlockSpec((w_in.shape[0], WIDTH), lambda i: (0, index))


def project_kernel(place, crossing, home, tokens, grad, w_query, w_out, key_tokens, w_key, w_value, packs, *refs):
    slices, refs = refs[:HEADS], refs[HEADS:]
    outs, (keys, values) = refs[:HEADS], refs[HEADS:]
    lane = lax.broadcasted_iota(jnp.int32, (MASK_ROWS, 2 * DH), 1)
    row = lax.broadcasted_iota(jnp.int32, (MASK_ROWS, 2 * DH), 0)
    mask = jnp.zeros((MASK_ROWS, 2 * DH), F32)
    for j in range(crossing.shape[1]):
        bit = jnp.where((crossing[0, j] > 0) | (home[0] == j), 1.0, 0.0)
        mask = jnp.where((lane == j) & (row == 0), bit, mask)
    for half, product in enumerate((mm(tokens[...], w_query[...], NN), mm(grad[...], w_out[...], NT))):
        product = product.astype(BF16)
        for h in range(HEADS):
            packs[h * PACK : h * PACK + BLOCK, half * DH : (half + 1) * DH] = product[:, h * DH : (h + 1) * DH]
    part = tokens.shape[1] // HEADS
    for d in range(HEADS):
        packs[d * PACK + BLOCK : (d + 1) * PACK, :] = mask.astype(BF16)
        columns = columns_of(lax.rem(place[0] + d, HEADS), part)
        slices[d][:, :part] = tokens[:, columns]
        slices[d][:, part:] = grad[:, columns]
    keys[...] = mm(key_tokens[...], w_key[...], NN).astype(BF16)
    values[...] = mm(key_tokens[...], w_value[...], NN).astype(BF16)
    for d in range(HEADS):
        head = columns_of(lax.rem(place[1] + d, HEADS), DH)
        outs[d][:, :DH] = keys[:, head]
        outs[d][:, DH:] = values[:, head]


def project(place, query_tokens, key_tokens, out_grad, w_in, w_out, crossing, home):
    rows, width = query_tokens.shape
    count = key_tokens.shape[0]
    results = call(
        project_kernel,
        [shape(HEADS * PACK, 2 * DH)]
        + [shape(rows, 2 * width // HEADS)] * HEADS
        + [shape(count, 2 * DH)] * HEADS,
        (place, crossing, home, query_tokens, out_grad, w_in, w_out, key_tokens, w_in, w_in),
        4 * (rows + count) * width * WIDTH,
        scratch=[pltpu.VMEM((count, WIDTH), BF16)] * 2,
        in_specs=[SMEM] * 3
        + [whole(query_tokens), whole(out_grad), third(w_in, 0), whole(w_out)]
        + [whole(key_tokens), third(w_in, 1), third(w_in, 2)],
    )
    return results[0], results[1 : HEADS + 1], results[HEADS + 1 :]


def side_kernel(place, key_tokens, *refs):
    slices, side = refs[:HEADS], refs[HEADS]
    rows, width = slices[0].shape
    for d in range(HEADS):
        side[d * rows : (d + 1) * rows, :width] = slices[d][...]
    part = width // 2
    side[:, width:] = key_tokens[:, columns_of(place[0], part)]


def joined(place, key_tokens, slices):
    width = 3 * key_tokens.shape[1] // HEADS
    return call(side_kernel, shape(key_tokens.shape[0], width), (place, key_tokens, *slices), 0)


def attend(place, packs, kv, ready, back, scores, bias, q_all, g_all, emit):
    keys, count = scores.shape
    chunk = keys // HEADS
    tiles = chunk // BLOCK
    scale = 1.0 / math.sqrt(DH)
    ones = jnp.ones((MASK_ROWS, BLOCK), BF16)
    for d in range(HEADS):
        rows = slice(d * BLOCK, (d + 1) * BLOCK)
        q_all[rows, :] = packs[d * PACK : d * PACK + BLOCK, :DH]
        g_all[rows, :] = packs[d * PACK : d * PACK + BLOCK, DH:]
        allowed = mm(packs[d * PACK + BLOCK : (d + 1) * PACK, :DH], ones, TN)
        bias[:, rows] = (allowed - 1.0) * 1e30
    q = q_all[...]
    g = g_all[...]
    best = jnp.full((1, count), -3e38, F32)
    for c in range(HEADS):
        ready(c)
        first = lax.rem(place[1] - c + HEADS, HEADS) * tiles
        raw = mm(kv[c * chunk : (c + 1) * chunk, :DH], q, NT)
        for j in range(tiles):
            tile = raw[j * BLOCK : (j + 1) * BLOCK, :] + bias[pl.ds(first + j, 1), :]
            scores[c * chunk + j * BLOCK : c * chunk + (j + 1) * BLOCK, :] = tile
            best = jnp.maximum(best, jnp.max(tile, axis=0, keepdims=True))
    total = jnp.zeros((1, count), F32)
    summed = jnp.zeros((DH, count), F32)
    for c in range(HEADS):
        part = slice(c * chunk, (c + 1) * chunk)
        weights = jnp.exp2((scores[part, :] - best) * (scale * math.log2(math.e)))
        scores[part, :] = weights
        total = total + jnp.sum(weights, axis=0, keepdims=True)
        summed = summed + mm(kv[part, DH:], weights.astype(BF16), TN)
    share = 1.0 / total
    attended = (summed * share).astype(BF16)
    spread = jnp.sum(jnp.transpose(g.astype(F32)) * attended.astype(F32), axis=0, keepdims=True)
    back[:, :DH] = jnp.transpose(attended.astype(F32)).astype(BF16)
    query_sum = jnp.zeros((DH, count), F32)
    for c in range(HEADS):
        part = slice(c * chunk, (c + 1) * chunk)
        probs = scores[part, :] * share
        grad_probs = mm(kv[part, DH:], g, NT)
        slope = (probs * (grad_probs - spread)).astype(BF16)
        emit(c, part, mm(slope, q, NN), mm(probs.astype(BF16), g, NN))
        query_sum = query_sum + mm(kv[part, :DH], slope, TN)
    back[:, DH:] = (jnp.transpose(query_sum) * scale).astype(BF16)


def chunk_copies(sources, targets, sems):
    return [pltpu.make_async_copy(a, b, sems.at[i]) for i, (a, b) in enumerate(zip(sources, targets))]


def chunks_of(ref):
    rows = ref.shape[0] // HEADS
    return [ref.at[c * rows : (c + 1) * rows, :] for c in range(HEADS)]


def planes_kernel(planes, place, *refs):
    packs, refs = refs[:planes], refs[planes:]
    kvs, refs = refs[:HEADS], refs[HEADS:]
    backs, refs = refs[:planes], refs[planes:]
    total, scores, bias, q_all, g_all, kv, sums, load_sems, store_sems = refs
    loads = chunk_copies(kvs, chunks_of(kv), load_sems)
    stores = chunk_copies(chunks_of(sums), chunks_of(total), store_sems)
    for copy in loads:
        copy.start()
    for i in range(planes):

        def ready(c):
            if i == 0:
                loads[c].wait()

        def emit(c, rows, key_step, value_step):
            if i == 0:
                sums[rows, :DH] = key_step
                sums[rows, DH:] = value_step
            else:
                sums[rows, :DH] += key_step
                sums[rows, DH:] += value_step
            if i == planes - 1:
                stores[c].start()

        attend(place, packs[i], kv, ready, backs[i], scores, bias, q_all, g_all, emit)
    for copy in stores:
        copy.wait()


def last_kernel(place, packs, *refs):
    kvs, refs = refs[:HEADS], refs[HEADS:]
    even_hbm, odd_hbm, own_back, back, home_parts, scores, bias, q_all, g_all, kv, even, odd, *sems = refs
    chunk = kvs[0].shape[0]
    scale = 1.0 / math.sqrt(DH)
    loads = chunk_copies(kvs, chunks_of(kv), sems[0])
    evens = chunk_copies(chunks_of(even_hbm), chunks_of(even), sems[1])
    odds = chunk_copies(chunks_of(odd_hbm), chunks_of(odd), sems[2])
    for copy in loads + evens + odds:
        copy.start()

    def ready(c):
        loads[c].wait()

    def emit(c, rows, key_step, value_step):
        evens[c].wait()
        odds[c].wait()
        start = lax.rem(place[1] - c + HEADS, HEADS) * (chunk + BLOCK)
        out = pl.ds(pl.multiple_of(start, BLOCK), chunk)
        key_sum = (even[rows, :DH] + key_step) + odd[rows, :DH]
        home_parts[out, :DH] = (key_sum * scale).astype(BF16)
        home_parts[out, DH:] = ((even[rows, DH:] + value_step) + odd[rows, DH:]).astype(BF16)

    attend(place, packs, kv, ready, back, scores, bias, q_all, g_all, emit)
    for h in range(HEADS):
        start = h * (chunk + BLOCK) + chunk
        home_parts[start : start + BLOCK, :] = own_back[h * BLOCK : (h + 1) * BLOCK, :]


def attention_scratch(kvs):
    keys = HEADS * kvs[0].shape[0]
    count = HEADS * BLOCK
    return [
        pltpu.VMEM((keys, count), F32),
        pltpu.VMEM((BLOCK, count), F32),
        pltpu.VMEM((count, DH), BF16),
        pltpu.VMEM((count, DH), BF16),
        pltpu.VMEM((keys, 2 * DH), BF16),
        pltpu.VMEM((keys, 2 * DH), F32),
    ]


def plane_attention(place, packs, kvs):
    planes = len(packs)
    keys = HEADS * kvs[0].shape[0]
    count = HEADS * BLOCK
    backs = [shape(count, 2 * DH)] * planes
    *backs, total = call(
        functools.partial(planes_kernel, planes),
        backs + [shape(keys, 2 * DH, F32)],
        (place, *packs, *kvs),
        12 * planes * keys * count * DH,
        scratch=attention_scratch(kvs) + [pltpu.SemaphoreType.DMA((HEADS,))] * 2,
        in_specs=[SMEM] + [whole(x) for x in packs] + [ANY] * HEADS,
        out_specs=[whole(x) for x in backs] + [ANY],
    )
    return backs, total


def last_attention(place, packs, kvs, even, odd, own_back):
    chunk = kvs[0].shape[0]
    keys = HEADS * chunk
    count = HEADS * BLOCK
    return call(
        last_kernel,
        [shape(count, 2 * DH), shape(HEADS * (chunk + BLOCK), 2 * DH)],
        (place, packs, *kvs, even, odd, own_back),
        12 * keys * count * DH,
        scratch=attention_scratch(kvs)
        + [pltpu.VMEM((keys, 2 * DH), F32)]
        + [pltpu.SemaphoreType.DMA((HEADS,))] * 3,
        in_specs=[SMEM, whole(packs)] + [ANY] * (HEADS + 2) + [whole(own_back)],
    )


def weights_kernel(place, home_parts, *refs):
    backs, refs = refs[:HEADS], refs[HEADS:]
    sides, (inner, outer) = refs[:HEADS], refs[HEADS:]
    part = inner.shape[0]
    chunk = sides[0].shape[0]
    for_keys, for_queries, for_output = 0.0, 0.0, 0.0
    for e in range(HEADS):
        soil = lax.rem(place[1] - e + HEADS, HEADS)
        rows = pl.ds(pl.multiple_of(soil * (chunk + BLOCK), BLOCK), chunk)
        for_keys = for_keys + mm(sides[e][:, 2 * part :], home_parts[rows, :], TN)
        block = columns_of(soil, BLOCK)
        right = jnp.concatenate([backs[d][block, :] for d in range(HEADS)], axis=0)
        for_queries = for_queries + mm(sides[e][:, :part], right[:, DH:], TN)
        for_output = for_output + mm(sides[e][:, part : 2 * part], right[:, :DH], TN)
    inner[:, : 2 * DH] = for_keys.astype(BF16)
    inner[:, 2 * DH :] = for_queries.astype(BF16)
    outer[...] = for_output.astype(BF16)


def weights_of(place, home_parts, backs, sides):
    part = sides[0].shape[1] // 3
    return call(
        weights_kernel,
        [shape(part, 3 * DH), shape(part, DH)],
        (place, home_parts, *backs, *sides),
        8 * HEADS * sides[0].shape[0] * part * DH,
    )


def home_kernel(parts, w_query, w_key, w_value, w_out, key_grad, output, query_grad):
    count = key_grad.shape[0]
    chunks = [parts.at[h * (count + BLOCK) : (h + 1) * (count + BLOCK), :] for h in range(HEADS)]
    keys = jnp.concatenate([x[:count, :DH] for x in chunks], axis=1)
    values = jnp.concatenate([x[:count, DH:] for x in chunks], axis=1)
    key_grad[...] = (mm(keys, w_key[...], NT) + mm(values, w_value[...], NT)).astype(BF16)
    attended = jnp.concatenate([x[count:, :DH] for x in chunks], axis=1)
    output[...] = mm(attended, w_out[...], NN).astype(BF16)
    grad = jnp.concatenate([x[count:, DH:] for x in chunks], axis=1)
    query_grad[...] = mm(grad, w_query[...], NT).astype(BF16)


def home_outputs(parts, w_in, w_out):
    width = w_in.shape[0]
    count = parts.shape[0] // HEADS - BLOCK
    return call(
        home_kernel,
        [shape(count, width), shape(BLOCK, width), shape(BLOCK, width)],
        (parts, w_in, w_in, w_in, w_out),
        4 * (count + BLOCK) * width * WIDTH,
        in_specs=[whole(parts), third(w_in, 0), third(w_in, 1), third(w_in, 2), whole(w_out)],
    )


def place_weights_kernel(place, *refs):
    inner, outer, (w_in_grad, w_out_grad) = refs[:HEADS], refs[HEADS : 2 * HEADS], refs[2 * HEADS :]
    rows = inner[0].shape[0]
    for d in range(HEADS):
        index = lax.rem(place[0] - d + HEADS, HEADS)
        w_in_grad[:, columns_of(index, DH)] = inner[d][:, 2 * DH :].astype(F32)
        w_in_grad[:, columns_of(HEADS + index, DH)] = inner[d][:, :DH].astype(F32)
        w_in_grad[:, columns_of(2 * HEADS + index, DH)] = inner[d][:, DH : 2 * DH].astype(F32)
        w_out_grad[:, columns_of(index, rows)] = jnp.transpose(outer[d][...].astype(F32))


def place_weights(place, inner, outer):
    rows = inner[0].shape[0]
    return call(
        place_weights_kernel,
        [shape(rows, 3 * WIDTH, F32), shape(DH, HEADS * rows, F32)],
        (place, *inner, *outer),
        rows * 4 * WIDTH,
    )


def after(value, *others):
    return lax.optimization_barrier((value, *others))[0]


def swapped(block, axis):
    return lax.all_to_all(block, axis, 0, 0, tiled=True)


def spread_to(block, axis):
    return [block] + [sent(block, axis, d) for d in range(1, HEADS)]


def head_body(query_tokens, key_tokens, w_in, w_out, out_grad, crossing, home):
    place = jnp.stack([lax.axis_index("stand"), lax.axis_index("soil")]).astype(jnp.int32)
    distances = range(1, HEADS)
    packs, slices, kvs = project(place, query_tokens, key_tokens, out_grad, w_in, w_out, crossing, home)
    packs = swapped(packs, "soil")
    kvs = [kvs[0]] + [sent(kvs[d], "soil", d) for d in distances]
    slices = [slices[0]] + [sent(slices[d], "stand", d) for d in distances]
    planes = spread_to(packs, "stand")
    sides = spread_to(joined(place, key_tokens, slices), "soil")
    (back_0,), even = plane_attention(place, planes[:1], kvs)
    (back_1, back_3), odd = plane_attention(place, [planes[1], planes[3]], kvs)
    back_2, home_parts = last_attention(place, planes[2], kvs, even, odd, back_0)
    inner, outer = weights_of(place, home_parts, [back_0, back_1, back_2, back_3], sides)
    home_parts = swapped(home_parts, "soil")
    key_grad, output, query_grad = home_outputs(home_parts, w_in, w_out)
    outer = spread_to(outer, "stand")
    crosswise = []
    for d in range(HEADS):
        route = [
            (soil * HEADS + stand, stand * HEADS + (soil + d) % HEADS)
            for stand in range(HEADS)
            for soil in range(HEADS)
        ]
        crosswise.append(lax.ppermute(inner, ("soil", "stand"), route))
    crosswise[0] = after(crosswise[0], key_grad)
    w_in_grad, w_out_grad = place_weights(place, crosswise, outer)
    return (output, query_grad, key_grad, w_in_grad, w_out_grad)


NEG = -1e30


def from_behind(block, axis, distance):
    devices = range(lax.axis_size(axis))
    route = [((i - distance) % len(devices), i) for i in devices]
    return lax.ppermute(block, axis, route)


def tile_mask(allowed, offset, columns):
    key_blocks = allowed.shape[1]
    column_block = (offset + jnp.arange(columns, dtype=jnp.int32)) // BLOCK
    onehot = (jnp.arange(key_blocks, dtype=jnp.int32)[:, None] == column_block[None, :]).astype(
        jnp.float32
    )
    coarse = jnp.dot(allowed, onehot)
    expanded = jnp.broadcast_to(coarse[:, None, :], (coarse.shape[0], BLOCK, columns))
    return expanded.reshape(coarse.shape[0] * BLOCK, columns)


def guarded_update(update, allowed_mask, operands, carried):
    return update(*operands, allowed_mask, carried)


def forward_tile(queries, key_proj, values, allowed_mask, carried):
    row_best, row_total, summed = carried
    query_count = queries.shape[0]
    key_count = key_proj.shape[0]
    query_heads = queries.reshape(query_count, HEADS, DH)
    key_heads = key_proj.reshape(key_count, HEADS, DH)
    value_heads = values.reshape(key_count, HEADS, DH)
    scores = jnp.einsum(
        "qhd,khd->hqk", query_heads, key_heads, preferred_element_type=jnp.float32
    ) * (1.0 / math.sqrt(DH))
    guarded = jnp.where(allowed_mask[None, :, :] > 0, scores, NEG)
    new_best = jnp.maximum(row_best, jnp.max(guarded, axis=2))
    rescale = jnp.exp(row_best - new_best)
    weights = jnp.exp(guarded - new_best[:, :, None]) * allowed_mask[None, :, :]
    row_total = row_total * rescale + jnp.sum(weights, axis=2)
    contrib = jnp.einsum(
        "hqk,khd->qhd",
        weights.astype(jnp.bfloat16),
        value_heads,
        preferred_element_type=jnp.float32,
    )
    summed = summed.reshape(query_count, HEADS, DH) * rescale.T[:, :, None] + contrib
    return (new_best, row_total, summed.reshape(query_count, HEADS * DH))


def backward_tile(queries, grad_att, log_total, spread, key_proj, values, allowed_mask, carried):
    grad_query, grad_key, grad_value = carried
    query_count = queries.shape[0]
    key_count = key_proj.shape[0]
    query_heads = queries.reshape(query_count, HEADS, DH)
    grad_heads = grad_att.reshape(query_count, HEADS, DH)
    key_heads = key_proj.reshape(key_count, HEADS, DH)
    value_heads = values.reshape(key_count, HEADS, DH)
    score_scale = 1.0 / math.sqrt(DH)
    scores = (
        jnp.einsum("qhd,khd->hqk", query_heads, key_heads, preferred_element_type=jnp.float32)
        * score_scale
    )
    probs = jnp.exp(jnp.where(allowed_mask[None, :, :] > 0, scores - log_total[:, :, None], NEG))
    grad_probs = jnp.einsum(
        "qhd,khd->hqk", grad_heads, value_heads, preferred_element_type=jnp.float32
    )
    grad_scores = (probs * (grad_probs - spread[:, :, None])).astype(jnp.bfloat16)
    query_step = (
        jnp.einsum("hqk,khd->qhd", grad_scores, key_heads, preferred_element_type=jnp.float32)
        * score_scale
    )
    key_step = (
        jnp.einsum("hqk,qhd->khd", grad_scores, query_heads, preferred_element_type=jnp.float32)
        * score_scale
    )
    value_step = jnp.einsum(
        "hqk,qhd->khd", probs.astype(jnp.bfloat16), grad_heads, preferred_element_type=jnp.float32
    )
    grad_query = grad_query + query_step.reshape(query_count, HEADS * DH)
    grad_key = grad_key + key_step.reshape(key_count, HEADS * DH)
    grad_value = grad_value + value_step.reshape(key_count, HEADS * DH)
    return (grad_query, grad_key, grad_value)


def ring_body(query_tokens, key_tokens, w_in, w_out, out_grad, crossing, home):
    attn_width = HEADS * DH
    query_count = query_tokens.shape[0]
    key_count = key_tokens.shape[0]
    soil_count = lax.axis_size("soil")
    soil_index = lax.axis_index("soil")
    stand_count = lax.axis_size("stand")
    stand_index = lax.axis_index("stand")
    total_blocks = key_count * soil_count // BLOCK
    allowed = (
        (crossing > 0) | (home[:, None] == jnp.arange(total_blocks, dtype=jnp.int32)[None, :])
    ).astype(jnp.float32)
    queries = jnp.dot(
        query_tokens, w_in[:, :attn_width], preferred_element_type=jnp.float32
    ).astype(jnp.bfloat16)
    projected = jnp.dot(
        key_tokens, w_in[:, attn_width:], preferred_element_type=jnp.float32
    ).astype(jnp.bfloat16)
    key_proj = projected[:, :attn_width]
    values = projected[:, attn_width:]
    key_offset = soil_index * key_count
    start_state = (
        jnp.full((HEADS, query_count), NEG, jnp.float32),
        jnp.zeros((HEADS, query_count), jnp.float32),
        jnp.zeros((query_count, attn_width), jnp.float32),
    )

    def forward_turn(turn_index, carried):
        moving, running = carried
        allowed_mask = tile_mask(moving[1].astype(jnp.float32), key_offset, key_count)
        running = guarded_update(forward_tile, allowed_mask, (moving[0], key_proj, values), running)
        moving = from_behind((moving[0], moving[1]), "soil", 1)
        running = from_behind(running, "soil", 1)
        return (moving, running)

    moving, running = lax.fori_loop(
        0, soil_count, forward_turn, ((queries, allowed.astype(jnp.bfloat16)), start_state)
    )
    row_best, row_total, summed = running
    attended = (
        (summed.reshape(query_count, HEADS, DH) / row_total.T[:, :, None])
        .reshape(query_count, attn_width)
        .astype(jnp.bfloat16)
    )
    log_total = row_best + jnp.log(row_total)
    output = jnp.dot(attended, w_out, preferred_element_type=jnp.float32).astype(jnp.bfloat16)
    grad_attended = lax.dot_general(
        out_grad, w_out, (((1,), (1,)), ((), ())), preferred_element_type=jnp.float32
    ).astype(jnp.bfloat16)
    spread = jnp.sum(
        (grad_attended.astype(jnp.float32) * attended.astype(jnp.float32)).reshape(
            query_count, HEADS, DH
        ),
        axis=2,
    ).T
    zero_query = jnp.zeros((query_count, attn_width), jnp.float32)
    zero_key = jnp.zeros((key_count, attn_width), jnp.float32)

    def backward_turn(turn_index, carried):
        moving, query_stats, grad_key, grad_value = carried
        allowed_mask = tile_mask(moving[2].astype(jnp.float32), key_offset, key_count)
        grad_query, grad_key, grad_value = guarded_update(
            backward_tile,
            allowed_mask,
            (moving[0], moving[1], query_stats[0], query_stats[1], key_proj, values),
            (query_stats[2], grad_key, grad_value),
        )
        moving = from_behind((moving[0], moving[1], moving[2]), "soil", 1)
        query_stats = from_behind((query_stats[0], query_stats[1], grad_query), "soil", 1)
        return (moving, query_stats, grad_key, grad_value)

    moving, query_stats, grad_key, grad_value = lax.fori_loop(
        0,
        soil_count,
        backward_turn,
        (
            (queries, grad_attended, allowed.astype(jnp.bfloat16)),
            (log_total, spread, zero_query),
            zero_key,
            zero_key,
        ),
    )
    grad_query = query_stats[2]
    grad_key, grad_value = lax.psum((grad_key, grad_value), "stand")
    key_grad_in = jnp.concatenate([grad_key, grad_value], axis=1).astype(jnp.bfloat16)
    query_grad_in = grad_query.astype(jnp.bfloat16)
    query_grad = lax.dot_general(
        query_grad_in,
        w_in[:, :attn_width],
        (((1,), (1,)), ((), ())),
        preferred_element_type=jnp.float32,
    ).astype(jnp.bfloat16)
    key_grad = lax.dot_general(
        key_grad_in,
        w_in[:, attn_width:],
        (((1,), (1,)), ((), ())),
        preferred_element_type=jnp.float32,
    ).astype(jnp.bfloat16)
    stand_rows = key_count // stand_count
    key_slice = lax.dynamic_slice_in_dim(key_tokens, stand_index * stand_rows, stand_rows, 0)
    grad_slice = lax.dynamic_slice_in_dim(key_grad_in, stand_index * stand_rows, stand_rows, 0)
    query_part = lax.dot_general(
        query_tokens, query_grad_in, (((0,), (0,)), ((), ())), preferred_element_type=jnp.float32
    )
    key_part = lax.dot_general(
        key_slice, grad_slice, (((0,), (0,)), ((), ())), preferred_element_type=jnp.float32
    )
    w_in_part = lax.psum_scatter(
        jnp.concatenate([query_part, key_part], axis=1), "soil", scatter_dimension=0, tiled=True
    )
    w_out_part = lax.psum_scatter(
        lax.dot_general(
            attended, out_grad, (((0,), (0,)), ((), ())), preferred_element_type=jnp.float32
        ),
        "soil",
        scatter_dimension=0,
        tiled=True,
    )
    w_in_grad, w_out_grad = lax.psum((w_in_part, w_out_part), "stand")
    return (output, query_grad, key_grad, w_in_grad, w_out_grad)


def solution(mesh):
    in_specs = (
        P(("field", "stand", "soil"), None),
        P(("field", "soil"), None),
        P(),
        P(),
        P(("field", "stand", "soil"), None),
        P(("field", "stand", "soil"), None),
        P(("field", "stand", "soil")),
    )
    out_specs = (
        P(("field", "stand", "soil"), None),
        P(("field", "stand", "soil"), None),
        P(("field", "soil"), None),
        P(("field", "soil"), None),
        P(("field", "soil"), None),
    )
    square = mesh.shape["stand"] == HEADS and mesh.shape["soil"] == HEADS
    body = head_body if square else ring_body
    return jax.shard_map(body, mesh=mesh, in_specs=in_specs, out_specs=out_specs, check_vma=False)
```

```python
import functools
import math

import jax
import jax.numpy as jnp
from jax import lax
from jax.experimental import pallas as pl
from jax.experimental.pallas import tpu as pltpu
from jax.sharding import PartitionSpec as P

HEADS = 4
DH = 128
BLOCK = 128
MASK_ROWS = 16
PACK = BLOCK + MASK_ROWS
LIMIT = 60
WIDTH = HEADS * DH
F32 = jnp.float32
BF16 = jnp.bfloat16
NT = (((1,), (1,)), ((), ()))
TN = (((0,), (0,)), ((), ()))
NN = (((1,), (0,)), ((), ()))


def mm(a, b, dims):
    return lax.dot_general(a, b, dims, preferred_element_type=F32)


def shape(rows, columns, dtype=BF16):
    return jax.ShapeDtypeStruct((rows, columns), dtype)


SMEM = pl.BlockSpec(memory_space=pltpu.SMEM)
ANY = pl.BlockSpec(memory_space=pl.ANY)


def columns_of(index, width):
    return pl.ds(pl.multiple_of(index * width, width), width)


def step_from(axis, distance):
    size = lax.axis_size(axis)
    return [((i - distance) % size, i) for i in range(size)]


def sent(block, axis, distance):
    return lax.ppermute(block, axis, step_from(axis, distance))


def whole(block):
    return pl.BlockSpec(block.shape, lambda *_: (0,) * len(block.shape))


def call(kernel, out_shape, operands, flops, scratch=(), in_specs=None, out_specs=None):
    if in_specs is None:
        in_specs = [SMEM if x.dtype == jnp.int32 else whole(x) for x in operands]
    outs = jax.tree.leaves(out_shape)
    traffic = sum(2 * math.prod(x.shape) for x in (*operands, *outs))
    return pl.pallas_call(
        kernel,
        out_shape=out_shape,
        grid=(1,),
        in_specs=in_specs,
        out_specs=jax.tree.map(whole, out_shape) if out_specs is None else out_specs,
        scratch_shapes=list(scratch),
        compiler_params=pltpu.CompilerParams(vmem_limit_bytes=LIMIT << 20),
        cost_estimate=pl.CostEstimate(flops=flops, bytes_accessed=traffic, transcendentals=0),
    )(*operands)


def third(w_in, index):
    return pl.BlockSpec((w_in.shape[0], WIDTH), lambda i: (0, index))


def project_kernel(place, crossing, home, tokens, grad, w_query, w_out, key_tokens, w_key, w_value, packs, *refs):
    slices, refs = refs[:HEADS], refs[HEADS:]
    outs, (keys, values) = refs[:HEADS], refs[HEADS:]
    lane = lax.broadcasted_iota(jnp.int32, (MASK_ROWS, 2 * DH), 1)
    row = lax.broadcasted_iota(jnp.int32, (MASK_ROWS, 2 * DH), 0)
    mask = jnp.zeros((MASK_ROWS, 2 * DH), F32)
    for j in range(crossing.shape[1]):
        bit = jnp.where((crossing[0, j] > 0) | (home[0] == j), 1.0, 0.0)
        mask = jnp.where((lane == j) & (row == 0), bit, mask)
    for half, product in enumerate((mm(tokens[...], w_query[...], NN), mm(grad[...], w_out[...], NT))):
        product = product.astype(BF16)
        for h in range(HEADS):
            packs[h * PACK : h * PACK + BLOCK, half * DH : (half + 1) * DH] = product[:, h * DH : (h + 1) * DH]
    part = tokens.shape[1] // HEADS
    for d in range(HEADS):
        packs[d * PACK + BLOCK : (d + 1) * PACK, :] = mask.astype(BF16)
        columns = columns_of(lax.rem(place[0] + d, HEADS), part)
        slices[d][:, :part] = tokens[:, columns]
        slices[d][:, part:] = grad[:, columns]
    keys[...] = mm(key_tokens[...], w_key[...], NN).astype(BF16)
    values[...] = mm(key_tokens[...], w_value[...], NN).astype(BF16)
    for d in range(HEADS):
        head = columns_of(lax.rem(place[1] + d, HEADS), DH)
        outs[d][:, :DH] = keys[:, head]
        outs[d][:, DH:] = values[:, head]


def project(place, query_tokens, key_tokens, out_grad, w_in, w_out, crossing, home):
    rows, width = query_tokens.shape
    count = key_tokens.shape[0]
    results = call(
        project_kernel,
        [shape(HEADS * PACK, 2 * DH)]
        + [shape(rows, 2 * width // HEADS)] * HEADS
        + [shape(count, 2 * DH)] * HEADS,
        (place, crossing, home, query_tokens, out_grad, w_in, w_out, key_tokens, w_in, w_in),
        4 * (rows + count) * width * WIDTH,
        scratch=[pltpu.VMEM((count, WIDTH), BF16)] * 2,
        in_specs=[SMEM] * 3
        + [whole(query_tokens), whole(out_grad), third(w_in, 0), whole(w_out)]
        + [whole(key_tokens), third(w_in, 1), third(w_in, 2)],
    )
    return results[0], results[1 : HEADS + 1], results[HEADS + 1 :]


def side_kernel(place, key_tokens, *refs):
    slices, side = refs[:HEADS], refs[HEADS]
    rows, width = slices[0].shape
    for d in range(HEADS):
        side[d * rows : (d + 1) * rows, :width] = slices[d][...]
    part = width // 2
    side[:, width:] = key_tokens[:, columns_of(place[0], part)]


def joined(place, key_tokens, slices):
    width = 3 * key_tokens.shape[1] // HEADS
    return call(side_kernel, shape(key_tokens.shape[0], width), (place, key_tokens, *slices), 0)


def attend(place, packs, kv, ready, back, scores, bias, q_all, g_all, emit):
    keys, count = scores.shape
    chunk = keys // HEADS
    tiles = chunk // BLOCK
    scale = 1.0 / math.sqrt(DH)
    ones = jnp.ones((MASK_ROWS, BLOCK), BF16)
    for d in range(HEADS):
        rows = slice(d * BLOCK, (d + 1) * BLOCK)
        q_all[rows, :] = packs[d * PACK : d * PACK + BLOCK, :DH]
        g_all[rows, :] = packs[d * PACK : d * PACK + BLOCK, DH:]
        allowed = mm(packs[d * PACK + BLOCK : (d + 1) * PACK, :DH], ones, TN)
        bias[:, rows] = (allowed - 1.0) * 1e30
    q = q_all[...]
    g = g_all[...]
    best = jnp.full((1, count), -3e38, F32)
    for c in range(HEADS):
        ready(c)
        first = lax.rem(place[1] - c + HEADS, HEADS) * tiles
        raw = mm(kv[c * chunk : (c + 1) * chunk, :DH], q, NT)
        for j in range(tiles):
            tile = raw[j * BLOCK : (j + 1) * BLOCK, :] + bias[pl.ds(first + j, 1), :]
            scores[c * chunk + j * BLOCK : c * chunk + (j + 1) * BLOCK, :] = tile
            best = jnp.maximum(best, jnp.max(tile, axis=0, keepdims=True))
    total = jnp.zeros((1, count), F32)
    summed = jnp.zeros((DH, count), F32)
    for c in range(HEADS):
        part = slice(c * chunk, (c + 1) * chunk)
        weights = jnp.exp2((scores[part, :] - best) * (scale * math.log2(math.e)))
        scores[part, :] = weights
        total = total + jnp.sum(weights, axis=0, keepdims=True)
        summed = summed + mm(kv[part, DH:], weights.astype(BF16), TN)
    share = 1.0 / total
    attended = (summed * share).astype(BF16)
    spread = jnp.sum(jnp.transpose(g.astype(F32)) * attended.astype(F32), axis=0, keepdims=True)
    back[:, :DH] = jnp.transpose(attended.astype(F32)).astype(BF16)
    query_sum = jnp.zeros((DH, count), F32)
    for c in range(HEADS):
        part = slice(c * chunk, (c + 1) * chunk)
        probs = scores[part, :] * share
        grad_probs = mm(kv[part, DH:], g, NT)
        slope = (probs * (grad_probs - spread)).astype(BF16)
        emit(c, part, mm(slope, q, NN), mm(probs.astype(BF16), g, NN))
        query_sum = query_sum + mm(kv[part, :DH], slope, TN)
    back[:, DH:] = (jnp.transpose(query_sum) * scale).astype(BF16)


def chunk_copies(sources, targets, sems):
    return [pltpu.make_async_copy(a, b, sems.at[i]) for i, (a, b) in enumerate(zip(sources, targets))]


def chunks_of(ref):
    rows = ref.shape[0] // HEADS
    return [ref.at[c * rows : (c + 1) * rows, :] for c in range(HEADS)]


def planes_kernel(planes, place, *refs):
    packs, refs = refs[:planes], refs[planes:]
    kvs, refs = refs[:HEADS], refs[HEADS:]
    backs, refs = refs[:planes], refs[planes:]
    total, scores, bias, q_all, g_all, kv, sums, load_sems, store_sems = refs
    loads = chunk_copies(kvs, chunks_of(kv), load_sems)
    stores = chunk_copies(chunks_of(sums), chunks_of(total), store_sems)
    for copy in loads:
        copy.start()
    for i in range(planes):

        def ready(c):
            if i == 0:
                loads[c].wait()

        def emit(c, rows, key_step, value_step):
            if i == 0:
                sums[rows, :DH] = key_step
                sums[rows, DH:] = value_step
            else:
                sums[rows, :DH] += key_step
                sums[rows, DH:] += value_step
            if i == planes - 1:
                stores[c].start()

        attend(place, packs[i], kv, ready, backs[i], scores, bias, q_all, g_all, emit)
    for copy in stores:
        copy.wait()


def last_kernel(place, packs, *refs):
    kvs, refs = refs[:HEADS], refs[HEADS:]
    even_hbm, odd_hbm, own_back, back, home_parts, scores, bias, q_all, g_all, kv, even, odd, *sems = refs
    chunk = kvs[0].shape[0]
    scale = 1.0 / math.sqrt(DH)
    loads = chunk_copies(kvs, chunks_of(kv), sems[0])
    evens = chunk_copies(chunks_of(even_hbm), chunks_of(even), sems[1])
    odds = chunk_copies(chunks_of(odd_hbm), chunks_of(odd), sems[2])
    for copy in loads + evens + odds:
        copy.start()

    def ready(c):
        loads[c].wait()

    def emit(c, rows, key_step, value_step):
        evens[c].wait()
        odds[c].wait()
        start = lax.rem(place[1] - c + HEADS, HEADS) * (chunk + BLOCK)
        out = pl.ds(pl.multiple_of(start, BLOCK), chunk)
        key_sum = (even[rows, :DH] + key_step) + odd[rows, :DH]
        home_parts[out, :DH] = (key_sum * scale).astype(BF16)
        home_parts[out, DH:] = ((even[rows, DH:] + value_step) + odd[rows, DH:]).astype(BF16)

    attend(place, packs, kv, ready, back, scores, bias, q_all, g_all, emit)
    for h in range(HEADS):
        start = h * (chunk + BLOCK) + chunk
        home_parts[start : start + BLOCK, :] = own_back[h * BLOCK : (h + 1) * BLOCK, :]


def attention_scratch(kvs):
    keys = HEADS * kvs[0].shape[0]
    count = HEADS * BLOCK
    return [
        pltpu.VMEM((keys, count), F32),
        pltpu.VMEM((BLOCK, count), F32),
        pltpu.VMEM((count, DH), BF16),
        pltpu.VMEM((count, DH), BF16),
        pltpu.VMEM((keys, 2 * DH), BF16),
        pltpu.VMEM((keys, 2 * DH), F32),
    ]


def plane_attention(place, packs, kvs):
    planes = len(packs)
    keys = HEADS * kvs[0].shape[0]
    count = HEADS * BLOCK
    backs = [shape(count, 2 * DH)] * planes
    *backs, total = call(
        functools.partial(planes_kernel, planes),
        backs + [shape(keys, 2 * DH, F32)],
        (place, *packs, *kvs),
        12 * planes * keys * count * DH,
        scratch=attention_scratch(kvs) + [pltpu.SemaphoreType.DMA((HEADS,))] * 2,
        in_specs=[SMEM] + [whole(x) for x in packs] + [ANY] * HEADS,
        out_specs=[whole(x) for x in backs] + [ANY],
    )
    return backs, total


def last_attention(place, packs, kvs, even, odd, own_back):
    chunk = kvs[0].shape[0]
    keys = HEADS * chunk
    count = HEADS * BLOCK
    return call(
        last_kernel,
        [shape(count, 2 * DH), shape(HEADS * (chunk + BLOCK), 2 * DH)],
        (place, packs, *kvs, even, odd, own_back),
        12 * keys * count * DH,
        scratch=attention_scratch(kvs)
        + [pltpu.VMEM((keys, 2 * DH), F32)]
        + [pltpu.SemaphoreType.DMA((HEADS,))] * 3,
        in_specs=[SMEM, whole(packs)] + [ANY] * (HEADS + 2) + [whole(own_back)],
    )


def weights_kernel(place, home_parts, *refs):
    backs, refs = refs[:HEADS], refs[HEADS:]
    sides, (inner, outer) = refs[:HEADS], refs[HEADS:]
    part = inner.shape[0]
    chunk = sides[0].shape[0]
    for_keys, for_queries, for_output = 0.0, 0.0, 0.0
    for e in range(HEADS):
        soil = lax.rem(place[1] - e + HEADS, HEADS)
        rows = pl.ds(pl.multiple_of(soil * (chunk + BLOCK), BLOCK), chunk)
        for_keys = for_keys + mm(sides[e][:, 2 * part :], home_parts[rows, :], TN)
        block = columns_of(soil, BLOCK)
        right = jnp.concatenate([backs[d][block, :] for d in range(HEADS)], axis=0)
        for_queries = for_queries + mm(sides[e][:, :part], right[:, DH:], TN)
        for_output = for_output + mm(sides[e][:, part : 2 * part], right[:, :DH], TN)
    inner[:, : 2 * DH] = for_keys.astype(BF16)
    inner[:, 2 * DH :] = for_queries.astype(BF16)
    outer[...] = for_output.astype(BF16)


def weights_of(place, home_parts, backs, sides):
    part = sides[0].shape[1] // 3
    return call(
        weights_kernel,
        [shape(part, 3 * DH), shape(part, DH)],
        (place, home_parts, *backs, *sides),
        8 * HEADS * sides[0].shape[0] * part * DH,
    )


def home_kernel(parts, w_query, w_key, w_value, w_out, key_grad, output, query_grad):
    count = key_grad.shape[0]
    chunks = [parts.at[h * (count + BLOCK) : (h + 1) * (count + BLOCK), :] for h in range(HEADS)]
    keys = jnp.concatenate([x[:count, :DH] for x in chunks], axis=1)
    values = jnp.concatenate([x[:count, DH:] for x in chunks], axis=1)
    key_grad[...] = (mm(keys, w_key[...], NT) + mm(values, w_value[...], NT)).astype(BF16)
    attended = jnp.concatenate([x[count:, :DH] for x in chunks], axis=1)
    output[...] = mm(attended, w_out[...], NN).astype(BF16)
    grad = jnp.concatenate([x[count:, DH:] for x in chunks], axis=1)
    query_grad[...] = mm(grad, w_query[...], NT).astype(BF16)


def home_outputs(parts, w_in, w_out):
    width = w_in.shape[0]
    count = parts.shape[0] // HEADS - BLOCK
    return call(
        home_kernel,
        [shape(count, width), shape(BLOCK, width), shape(BLOCK, width)],
        (parts, w_in, w_in, w_in, w_out),
        4 * (count + BLOCK) * width * WIDTH,
        in_specs=[whole(parts), third(w_in, 0), third(w_in, 1), third(w_in, 2), whole(w_out)],
    )


def place_weights_kernel(place, *refs):
    inner, outer, (w_in_grad, w_out_grad) = refs[:HEADS], refs[HEADS : 2 * HEADS], refs[2 * HEADS :]
    rows = inner[0].shape[0]
    for d in range(HEADS):
        index = lax.rem(place[0] - d + HEADS, HEADS)
        w_in_grad[:, columns_of(index, DH)] = inner[d][:, 2 * DH :].astype(F32)
        w_in_grad[:, columns_of(HEADS + index, DH)] = inner[d][:, :DH].astype(F32)
        w_in_grad[:, columns_of(2 * HEADS + index, DH)] = inner[d][:, DH : 2 * DH].astype(F32)
        w_out_grad[:, columns_of(index, rows)] = jnp.transpose(outer[d][...].astype(F32))


def place_weights(place, inner, outer):
    rows = inner[0].shape[0]
    return call(
        place_weights_kernel,
        [shape(rows, 3 * WIDTH, F32), shape(DH, HEADS * rows, F32)],
        (place, *inner, *outer),
        rows * 4 * WIDTH,
    )


def finish_kernel(place, *refs):
    pieces, refs = refs[: 2 * HEADS], refs[2 * HEADS :]
    home, (w_in_grad, w_out_grad) = (*refs[:5], *refs[7:]), refs[5:7]
    home_kernel(*home)
    place_weights_kernel(place, *pieces, w_in_grad, w_out_grad)


def finish(place, inner, outer, parts, w_in, w_out):
    rows = inner[0].shape[0]
    width = w_in.shape[0]
    count = parts.shape[0] // HEADS - BLOCK
    return call(
        finish_kernel,
        [
            shape(rows, 3 * WIDTH, F32),
            shape(DH, HEADS * rows, F32),
            shape(count, width),
            shape(BLOCK, width),
            shape(BLOCK, width),
        ],
        (place, *inner, *outer, parts, w_in, w_in, w_in, w_out),
        4 * (count + BLOCK) * width * WIDTH,
        in_specs=[SMEM]
        + [whole(x) for x in (*inner, *outer, parts)]
        + [third(w_in, 0), third(w_in, 1), third(w_in, 2), whole(w_out)],
    )


def after(value, *others):
    return lax.optimization_barrier((value, *others))[0]


def swapped(block, axis):
    return lax.all_to_all(block, axis, 0, 0, tiled=True)


def spread_to(block, axis):
    return [block] + [sent(block, axis, d) for d in range(1, HEADS)]


def head_body(query_tokens, key_tokens, w_in, w_out, out_grad, crossing, home):
    place = jnp.stack([lax.axis_index("stand"), lax.axis_index("soil")]).astype(jnp.int32)
    distances = range(1, HEADS)
    packs, slices, kvs = project(place, query_tokens, key_tokens, out_grad, w_in, w_out, crossing, home)
    packs = swapped(packs, "soil")
    kvs = [kvs[0]] + [sent(kvs[d], "soil", d) for d in distances]
    slices = [slices[0]] + [sent(slices[d], "stand", d) for d in distances]
    planes = spread_to(packs, "stand")
    side = joined(place, key_tokens, slices)
    sides = [side, sent(side, "soil", 1), sent(after(side, planes[1]), "soil", 2), sent(side, "soil", 3)]
    (back_0,), even = plane_attention(place, planes[:1], kvs)
    (back_1, back_3), odd = plane_attention(place, [planes[1], planes[3]], kvs)
    back_2, home_parts = last_attention(place, planes[2], kvs, even, odd, back_0)
    inner, outer = weights_of(place, home_parts, [back_0, back_1, back_2, back_3], sides)
    home_parts = swapped(home_parts, "soil")
    outer = spread_to(outer, "stand")
    crosswise = []
    for d in range(HEADS):
        route = [
            (soil * HEADS + stand, stand * HEADS + (soil + d) % HEADS)
            for stand in range(HEADS)
            for soil in range(HEADS)
        ]
        held = inner if d < 2 else after(inner, outer[d - 1])
        crosswise.append(lax.ppermute(held, ("soil", "stand"), route))
    results = finish(place, crosswise, outer, home_parts, w_in, w_out)
    w_in_grad, w_out_grad, key_grad, output, query_grad = results
    return (output, query_grad, key_grad, w_in_grad, w_out_grad)


NEG = -1e30


def from_behind(block, axis, distance):
    devices = range(lax.axis_size(axis))
    route = [((i - distance) % len(devices), i) for i in devices]
    return lax.ppermute(block, axis, route)


def tile_mask(allowed, offset, columns):
    key_blocks = allowed.shape[1]
    column_block = (offset + jnp.arange(columns, dtype=jnp.int32)) // BLOCK
    onehot = (jnp.arange(key_blocks, dtype=jnp.int32)[:, None] == column_block[None, :]).astype(
        jnp.float32
    )
    coarse = jnp.dot(allowed, onehot)
    expanded = jnp.broadcast_to(coarse[:, None, :], (coarse.shape[0], BLOCK, columns))
    return expanded.reshape(coarse.shape[0] * BLOCK, columns)


def guarded_update(update, allowed_mask, operands, carried):
    return update(*operands, allowed_mask, carried)


def forward_tile(queries, key_proj, values, allowed_mask, carried):
    row_best, row_total, summed = carried
    query_count = queries.shape[0]
    key_count = key_proj.shape[0]
    query_heads = queries.reshape(query_count, HEADS, DH)
    key_heads = key_proj.reshape(key_count, HEADS, DH)
    value_heads = values.reshape(key_count, HEADS, DH)
    scores = jnp.einsum(
        "qhd,khd->hqk", query_heads, key_heads, preferred_element_type=jnp.float32
    ) * (1.0 / math.sqrt(DH))
    guarded = jnp.where(allowed_mask[None, :, :] > 0, scores, NEG)
    new_best = jnp.maximum(row_best, jnp.max(guarded, axis=2))
    rescale = jnp.exp(row_best - new_best)
    weights = jnp.exp(guarded - new_best[:, :, None]) * allowed_mask[None, :, :]
    row_total = row_total * rescale + jnp.sum(weights, axis=2)
    contrib = jnp.einsum(
        "hqk,khd->qhd",
        weights.astype(jnp.bfloat16),
        value_heads,
        preferred_element_type=jnp.float32,
    )
    summed = summed.reshape(query_count, HEADS, DH) * rescale.T[:, :, None] + contrib
    return (new_best, row_total, summed.reshape(query_count, HEADS * DH))


def backward_tile(queries, grad_att, log_total, spread, key_proj, values, allowed_mask, carried):
    grad_query, grad_key, grad_value = carried
    query_count = queries.shape[0]
    key_count = key_proj.shape[0]
    query_heads = queries.reshape(query_count, HEADS, DH)
    grad_heads = grad_att.reshape(query_count, HEADS, DH)
    key_heads = key_proj.reshape(key_count, HEADS, DH)
    value_heads = values.reshape(key_count, HEADS, DH)
    score_scale = 1.0 / math.sqrt(DH)
    scores = (
        jnp.einsum("qhd,khd->hqk", query_heads, key_heads, preferred_element_type=jnp.float32)
        * score_scale
    )
    probs = jnp.exp(jnp.where(allowed_mask[None, :, :] > 0, scores - log_total[:, :, None], NEG))
    grad_probs = jnp.einsum(
        "qhd,khd->hqk", grad_heads, value_heads, preferred_element_type=jnp.float32
    )
    grad_scores = (probs * (grad_probs - spread[:, :, None])).astype(jnp.bfloat16)
    query_step = (
        jnp.einsum("hqk,khd->qhd", grad_scores, key_heads, preferred_element_type=jnp.float32)
        * score_scale
    )
    key_step = (
        jnp.einsum("hqk,qhd->khd", grad_scores, query_heads, preferred_element_type=jnp.float32)
        * score_scale
    )
    value_step = jnp.einsum(
        "hqk,qhd->khd", probs.astype(jnp.bfloat16), grad_heads, preferred_element_type=jnp.float32
    )
    grad_query = grad_query + query_step.reshape(query_count, HEADS * DH)
    grad_key = grad_key + key_step.reshape(key_count, HEADS * DH)
    grad_value = grad_value + value_step.reshape(key_count, HEADS * DH)
    return (grad_query, grad_key, grad_value)


def ring_body(query_tokens, key_tokens, w_in, w_out, out_grad, crossing, home):
    attn_width = HEADS * DH
    query_count = query_tokens.shape[0]
    key_count = key_tokens.shape[0]
    soil_count = lax.axis_size("soil")
    soil_index = lax.axis_index("soil")
    stand_count = lax.axis_size("stand")
    stand_index = lax.axis_index("stand")
    total_blocks = key_count * soil_count // BLOCK
    allowed = (
        (crossing > 0) | (home[:, None] == jnp.arange(total_blocks, dtype=jnp.int32)[None, :])
    ).astype(jnp.float32)
    queries = jnp.dot(
        query_tokens, w_in[:, :attn_width], preferred_element_type=jnp.float32
    ).astype(jnp.bfloat16)
    projected = jnp.dot(
        key_tokens, w_in[:, attn_width:], preferred_element_type=jnp.float32
    ).astype(jnp.bfloat16)
    key_proj = projected[:, :attn_width]
    values = projected[:, attn_width:]
    key_offset = soil_index * key_count
    start_state = (
        jnp.full((HEADS, query_count), NEG, jnp.float32),
        jnp.zeros((HEADS, query_count), jnp.float32),
        jnp.zeros((query_count, attn_width), jnp.float32),
    )

    def forward_turn(turn_index, carried):
        moving, running = carried
        allowed_mask = tile_mask(moving[1].astype(jnp.float32), key_offset, key_count)
        running = guarded_update(forward_tile, allowed_mask, (moving[0], key_proj, values), running)
        moving = from_behind((moving[0], moving[1]), "soil", 1)
        running = from_behind(running, "soil", 1)
        return (moving, running)

    moving, running = lax.fori_loop(
        0, soil_count, forward_turn, ((queries, allowed.astype(jnp.bfloat16)), start_state)
    )
    row_best, row_total, summed = running
    attended = (
        (summed.reshape(query_count, HEADS, DH) / row_total.T[:, :, None])
        .reshape(query_count, attn_width)
        .astype(jnp.bfloat16)
    )
    log_total = row_best + jnp.log(row_total)
    output = jnp.dot(attended, w_out, preferred_element_type=jnp.float32).astype(jnp.bfloat16)
    grad_attended = lax.dot_general(
        out_grad, w_out, (((1,), (1,)), ((), ())), preferred_element_type=jnp.float32
    ).astype(jnp.bfloat16)
    spread = jnp.sum(
        (grad_attended.astype(jnp.float32) * attended.astype(jnp.float32)).reshape(
            query_count, HEADS, DH
        ),
        axis=2,
    ).T
    zero_query = jnp.zeros((query_count, attn_width), jnp.float32)
    zero_key = jnp.zeros((key_count, attn_width), jnp.float32)

    def backward_turn(turn_index, carried):
        moving, query_stats, grad_key, grad_value = carried
        allowed_mask = tile_mask(moving[2].astype(jnp.float32), key_offset, key_count)
        grad_query, grad_key, grad_value = guarded_update(
            backward_tile,
            allowed_mask,
            (moving[0], moving[1], query_stats[0], query_stats[1], key_proj, values),
            (query_stats[2], grad_key, grad_value),
        )
        moving = from_behind((moving[0], moving[1], moving[2]), "soil", 1)
        query_stats = from_behind((query_stats[0], query_stats[1], grad_query), "soil", 1)
        return (moving, query_stats, grad_key, grad_value)

    moving, query_stats, grad_key, grad_value = lax.fori_loop(
        0,
        soil_count,
        backward_turn,
        (
            (queries, grad_attended, allowed.astype(jnp.bfloat16)),
            (log_total, spread, zero_query),
            zero_key,
            zero_key,
        ),
    )
    grad_query = query_stats[2]
    grad_key, grad_value = lax.psum((grad_key, grad_value), "stand")
    key_grad_in = jnp.concatenate([grad_key, grad_value], axis=1).astype(jnp.bfloat16)
    query_grad_in = grad_query.astype(jnp.bfloat16)
    query_grad = lax.dot_general(
        query_grad_in,
        w_in[:, :attn_width],
        (((1,), (1,)), ((), ())),
        preferred_element_type=jnp.float32,
    ).astype(jnp.bfloat16)
    key_grad = lax.dot_general(
        key_grad_in,
        w_in[:, attn_width:],
        (((1,), (1,)), ((), ())),
        preferred_element_type=jnp.float32,
    ).astype(jnp.bfloat16)
    stand_rows = key_count // stand_count
    key_slice = lax.dynamic_slice_in_dim(key_tokens, stand_index * stand_rows, stand_rows, 0)
    grad_slice = lax.dynamic_slice_in_dim(key_grad_in, stand_index * stand_rows, stand_rows, 0)
    query_part = lax.dot_general(
        query_tokens, query_grad_in, (((0,), (0,)), ((), ())), preferred_element_type=jnp.float32
    )
    key_part = lax.dot_general(
        key_slice, grad_slice, (((0,), (0,)), ((), ())), preferred_element_type=jnp.float32
    )
    w_in_part = lax.psum_scatter(
        jnp.concatenate([query_part, key_part], axis=1), "soil", scatter_dimension=0, tiled=True
    )
    w_out_part = lax.psum_scatter(
        lax.dot_general(
            attended, out_grad, (((0,), (0,)), ((), ())), preferred_element_type=jnp.float32
        ),
        "soil",
        scatter_dimension=0,
        tiled=True,
    )
    w_in_grad, w_out_grad = lax.psum((w_in_part, w_out_part), "stand")
    return (output, query_grad, key_grad, w_in_grad, w_out_grad)


def solution(mesh):
    in_specs = (
        P(("field", "stand", "soil"), None),
        P(("field", "soil"), None),
        P(),
        P(),
        P(("field", "stand", "soil"), None),
        P(("field", "stand", "soil"), None),
        P(("field", "stand", "soil")),
    )
    out_specs = (
        P(("field", "stand", "soil"), None),
        P(("field", "stand", "soil"), None),
        P(("field", "soil"), None),
        P(("field", "soil"), None),
        P(("field", "soil"), None),
    )
    square = mesh.shape["stand"] == HEADS and mesh.shape["soil"] == HEADS
    body = head_body if square else ring_body
    return jax.shard_map(body, mesh=mesh, in_specs=in_specs, out_specs=out_specs, check_vma=False)
```

```python
import functools
import math

import jax
import jax.numpy as jnp
from jax import lax
from jax.experimental import pallas as pl
from jax.experimental.pallas import tpu as pltpu
from jax.sharding import PartitionSpec as P

HEADS = 4
DH = 128
BLOCK = 128
MASK_ROWS = 16
PACK = BLOCK + MASK_ROWS
LIMIT = 60
WIDTH = HEADS * DH
F32 = jnp.float32
BF16 = jnp.bfloat16
NT = (((1,), (1,)), ((), ()))
TN = (((0,), (0,)), ((), ()))
NN = (((1,), (0,)), ((), ()))


def mm(a, b, dims):
    return lax.dot_general(a, b, dims, preferred_element_type=F32)


def shape(rows, columns, dtype=BF16):
    return jax.ShapeDtypeStruct((rows, columns), dtype)


SMEM = pl.BlockSpec(memory_space=pltpu.SMEM)
ANY = pl.BlockSpec(memory_space=pl.ANY)


def columns_of(index, width):
    return pl.ds(pl.multiple_of(index * width, width), width)


def step_from(axis, distance):
    size = lax.axis_size(axis)
    return [((i - distance) % size, i) for i in range(size)]


def sent(block, axis, distance):
    return lax.ppermute(block, axis, step_from(axis, distance))


def whole(block):
    return pl.BlockSpec(block.shape, lambda *_: (0,) * len(block.shape))


def call(kernel, out_shape, operands, flops, scratch=(), in_specs=None, out_specs=None):
    if operands[0] is None:
        body, operands, in_specs = kernel, operands[1:], in_specs and in_specs[1:]
        kernel = lambda *refs: body((lax.axis_index("stand"), lax.axis_index("soil")), *refs)
    if in_specs is None:
        in_specs = [SMEM if x.dtype == jnp.int32 else whole(x) for x in operands]
    outs = jax.tree.leaves(out_shape)
    traffic = sum(2 * math.prod(x.shape) for x in (*operands, *outs))
    return pl.pallas_call(
        kernel,
        out_shape=out_shape,
        grid=(1,),
        in_specs=in_specs,
        out_specs=jax.tree.map(whole, out_shape) if out_specs is None else out_specs,
        scratch_shapes=list(scratch),
        compiler_params=pltpu.CompilerParams(vmem_limit_bytes=LIMIT << 20),
        cost_estimate=pl.CostEstimate(flops=flops, bytes_accessed=traffic, transcendentals=0),
    )(*operands)


def third(w_in, index):
    return pl.BlockSpec((w_in.shape[0], WIDTH), lambda i: (0, index))


def project_kernel(place, crossing, home, tokens_hbm, grad_hbm, w_in_hbm, w_out_hbm, keys_hbm, packs, *refs):
    *refs, tokens, grad, w_query, w_out, key_tokens, w_key, w_value, sems = refs
    copies = [
        pltpu.make_async_copy(source, target, sems.at[i])
        for i, (source, target) in enumerate(
            (
                (tokens_hbm, tokens),
                (w_in_hbm.at[:, :WIDTH], w_query),
                (grad_hbm, grad),
                (w_out_hbm, w_out),
                (keys_hbm, key_tokens),
                (w_in_hbm.at[:, WIDTH : 2 * WIDTH], w_key),
                (w_in_hbm.at[:, 2 * WIDTH :], w_value),
            )
        )
    ]
    for copy in copies:
        copy.start()
    slices, refs = refs[:HEADS], refs[HEADS:]
    outs, (keys, values) = refs[:HEADS], refs[HEADS:]
    lane = lax.broadcasted_iota(jnp.int32, (MASK_ROWS, 2 * DH), 1)
    row = lax.broadcasted_iota(jnp.int32, (MASK_ROWS, 2 * DH), 0)
    mask = jnp.zeros((MASK_ROWS, 2 * DH), F32)
    for j in range(crossing.shape[1]):
        bit = jnp.where((crossing[0, j] > 0) | (home[0] == j), 1.0, 0.0)
        mask = jnp.where((lane == j) & (row == 0), bit, mask)
    for half, (left, right, dims) in enumerate(((tokens, w_query, NN), (grad, w_out, NT))):
        copies[2 * half].wait()
        copies[2 * half + 1].wait()
        product = mm(left[...], right[...], dims).astype(BF16)
        for h in range(HEADS):
            packs[h * PACK : h * PACK + BLOCK, half * DH : (half + 1) * DH] = product[:, h * DH : (h + 1) * DH]
    part = tokens.shape[1] // HEADS
    for d in range(HEADS):
        packs[d * PACK + BLOCK : (d + 1) * PACK, :] = mask.astype(BF16)
        columns = columns_of(lax.rem(place[0] + d, HEADS), part)
        slices[d][:, :part] = tokens[:, columns]
        slices[d][:, part:] = grad[:, columns]
    copies[4].wait()
    copies[5].wait()
    keys[...] = mm(key_tokens[...], w_key[...], NN).astype(BF16)
    copies[6].wait()
    values[...] = mm(key_tokens[...], w_value[...], NN).astype(BF16)
    for d in range(HEADS):
        head = columns_of(lax.rem(place[1] + d, HEADS), DH)
        outs[d][:, :DH] = keys[:, head]
        outs[d][:, DH:] = values[:, head]


def project(place, query_tokens, key_tokens, out_grad, w_in, w_out, crossing, home):
    rows, width = query_tokens.shape
    count = key_tokens.shape[0]
    results = call(
        project_kernel,
        [shape(HEADS * PACK, 2 * DH)]
        + [shape(rows, 2 * width // HEADS)] * HEADS
        + [shape(count, 2 * DH)] * HEADS,
        (place, crossing, home, query_tokens, out_grad, w_in, w_out, key_tokens),
        4 * (rows + count) * width * WIDTH,
        scratch=[pltpu.VMEM((count, WIDTH), BF16)] * 2
        + [pltpu.VMEM((rows, width), BF16)] * 2
        + [pltpu.VMEM((width, WIDTH), BF16), pltpu.VMEM((WIDTH, width), BF16)]
        + [pltpu.VMEM((count, width), BF16)]
        + [pltpu.VMEM((width, WIDTH), BF16)] * 2
        + [pltpu.SemaphoreType.DMA((7,))],
        in_specs=[SMEM] * 3 + [ANY] * 5,
    )
    return results[0], results[1 : HEADS + 1], results[HEADS + 1 :]


def side_kernel(place, key_tokens, *refs):
    slices, side = refs[:HEADS], refs[HEADS]
    rows, width = slices[0].shape
    for d in range(HEADS):
        side[d * rows : (d + 1) * rows, :width] = slices[d][...]
    part = width // 2
    side[:, width:] = key_tokens[:, columns_of(place[0], part)]


def joined(place, key_tokens, slices):
    width = 3 * key_tokens.shape[1] // HEADS
    return call(side_kernel, shape(key_tokens.shape[0], width), (place, key_tokens, *slices), 0)


def attend(place, packs, kv, ready, back, scores, bias, q_all, g_all, emit):
    keys, count = scores.shape
    chunk = keys // HEADS
    tiles = chunk // BLOCK
    scale = 1.0 / math.sqrt(DH)
    ones = jnp.ones((MASK_ROWS, BLOCK), BF16)
    for d in range(HEADS):
        rows = slice(d * BLOCK, (d + 1) * BLOCK)
        q_all[rows, :] = packs[d * PACK : d * PACK + BLOCK, :DH]
        g_all[rows, :] = packs[d * PACK : d * PACK + BLOCK, DH:]
        allowed = mm(packs[d * PACK + BLOCK : (d + 1) * PACK, :DH], ones, TN)
        bias[:, rows] = (allowed - 1.0) * 1e30
    q = q_all[...]
    g = g_all[...]
    best = jnp.full((1, count), -3e38, F32)
    for c in range(HEADS):
        ready(c)
        first = lax.rem(place[1] - c + HEADS, HEADS) * tiles
        raw = mm(kv[c * chunk : (c + 1) * chunk, :DH], q, NT)
        for j in range(tiles):
            tile = raw[j * BLOCK : (j + 1) * BLOCK, :] + bias[pl.ds(first + j, 1), :]
            scores[c * chunk + j * BLOCK : c * chunk + (j + 1) * BLOCK, :] = tile
            best = jnp.maximum(best, jnp.max(tile, axis=0, keepdims=True))
    total = jnp.zeros((1, count), F32)
    summed = jnp.zeros((DH, count), F32)
    for c in range(HEADS):
        part = slice(c * chunk, (c + 1) * chunk)
        weights = jnp.exp2((scores[part, :] - best) * (scale * math.log2(math.e)))
        scores[part, :] = weights
        total = total + jnp.sum(weights, axis=0, keepdims=True)
        summed = summed + mm(kv[part, DH:], weights.astype(BF16), TN)
    share = 1.0 / total
    attended = (summed * share).astype(BF16)
    spread = jnp.sum(jnp.transpose(g.astype(F32)) * attended.astype(F32), axis=0, keepdims=True)
    back[:, :DH] = jnp.transpose(attended.astype(F32)).astype(BF16)
    query_sum = jnp.zeros((DH, count), F32)
    for c in range(HEADS):
        part = slice(c * chunk, (c + 1) * chunk)
        probs = scores[part, :] * share
        grad_probs = mm(kv[part, DH:], g, NT)
        slope = (probs * (grad_probs - spread)).astype(BF16)
        emit(c, part, mm(slope, q, NN), mm(probs.astype(BF16), g, NN))
        query_sum = query_sum + mm(kv[part, :DH], slope, TN)
    back[:, DH:] = (jnp.transpose(query_sum) * scale).astype(BF16)


def chunk_copies(sources, targets, sems):
    return [pltpu.make_async_copy(a, b, sems.at[i]) for i, (a, b) in enumerate(zip(sources, targets))]


def chunks_of(ref):
    rows = ref.shape[0] // HEADS
    return [ref.at[c * rows : (c + 1) * rows, :] for c in range(HEADS)]


def planes_kernel(planes, place, *refs):
    packs, refs = refs[:planes], refs[planes:]
    kvs, refs = refs[:HEADS], refs[HEADS:]
    backs, refs = refs[:planes], refs[planes:]
    total, scores, bias, q_all, g_all, kv, sums, load_sems, store_sems = refs
    loads = chunk_copies(kvs, chunks_of(kv), load_sems)
    stores = chunk_copies(chunks_of(sums), chunks_of(total), store_sems)
    for copy in loads:
        copy.start()
    for i in range(planes):

        def ready(c):
            if i == 0:
                loads[c].wait()

        def emit(c, rows, key_step, value_step):
            if i == 0:
                sums[rows, :DH] = key_step
                sums[rows, DH:] = value_step
            else:
                sums[rows, :DH] += key_step
                sums[rows, DH:] += value_step
            if i == planes - 1:
                stores[c].start()

        attend(place, packs[i], kv, ready, backs[i], scores, bias, q_all, g_all, emit)
    for copy in stores:
        copy.wait()


def last_kernel(place, packs, *refs):
    kvs, refs = refs[:HEADS], refs[HEADS:]
    even_hbm, odd_hbm, own_back, back, home_parts, scores, bias, q_all, g_all, kv, even, odd, *sems = refs
    chunk = kvs[0].shape[0]
    scale = 1.0 / math.sqrt(DH)
    loads = chunk_copies(kvs, chunks_of(kv), sems[0])
    evens = chunk_copies(chunks_of(even_hbm), chunks_of(even), sems[1])
    odds = chunk_copies(chunks_of(odd_hbm), chunks_of(odd), sems[2])
    for copy in loads + evens + odds:
        copy.start()

    def ready(c):
        loads[c].wait()

    def emit(c, rows, key_step, value_step):
        evens[c].wait()
        odds[c].wait()
        start = lax.rem(place[1] - c + HEADS, HEADS) * (chunk + BLOCK)
        out = pl.ds(pl.multiple_of(start, BLOCK), chunk)
        key_sum = (even[rows, :DH] + key_step) + odd[rows, :DH]
        home_parts[out, :DH] = (key_sum * scale).astype(BF16)
        home_parts[out, DH:] = ((even[rows, DH:] + value_step) + odd[rows, DH:]).astype(BF16)

    attend(place, packs, kv, ready, back, scores, bias, q_all, g_all, emit)
    for h in range(HEADS):
        start = h * (chunk + BLOCK) + chunk
        home_parts[start : start + BLOCK, :] = own_back[h * BLOCK : (h + 1) * BLOCK, :]


def attention_scratch(kvs):
    keys = HEADS * kvs[0].shape[0]
    count = HEADS * BLOCK
    return [
        pltpu.VMEM((keys, count), F32),
        pltpu.VMEM((BLOCK, count), F32),
        pltpu.VMEM((count, DH), BF16),
        pltpu.VMEM((count, DH), BF16),
        pltpu.VMEM((keys, 2 * DH), BF16),
        pltpu.VMEM((keys, 2 * DH), F32),
    ]


def plane_attention(place, packs, kvs):
    planes = len(packs)
    keys = HEADS * kvs[0].shape[0]
    count = HEADS * BLOCK
    backs = [shape(count, 2 * DH)] * planes
    *backs, total = call(
        functools.partial(planes_kernel, planes),
        backs + [shape(keys, 2 * DH, F32)],
        (place, *packs, *kvs),
        12 * planes * keys * count * DH,
        scratch=attention_scratch(kvs) + [pltpu.SemaphoreType.DMA((HEADS,))] * 2,
        in_specs=[SMEM] + [whole(x) for x in packs] + [ANY] * HEADS,
        out_specs=[whole(x) for x in backs] + [ANY],
    )
    return backs, total


def last_attention(place, packs, kvs, even, odd, own_back):
    chunk = kvs[0].shape[0]
    keys = HEADS * chunk
    count = HEADS * BLOCK
    return call(
        last_kernel,
        [shape(count, 2 * DH), shape(HEADS * (chunk + BLOCK), 2 * DH)],
        (place, packs, *kvs, even, odd, own_back),
        12 * keys * count * DH,
        scratch=attention_scratch(kvs)
        + [pltpu.VMEM((keys, 2 * DH), F32)]
        + [pltpu.SemaphoreType.DMA((HEADS,))] * 3,
        in_specs=[SMEM, whole(packs)] + [ANY] * (HEADS + 2) + [whole(own_back)],
    )


def weights_kernel(place, home_parts, *refs):
    backs, refs = refs[:HEADS], refs[HEADS:]
    sides, (inner, outer) = refs[:HEADS], refs[HEADS:]
    part = inner.shape[0]
    chunk = sides[0].shape[0]
    for_keys, for_queries, for_output = 0.0, 0.0, 0.0
    for e in range(HEADS):
        soil = lax.rem(place[1] - e + HEADS, HEADS)
        rows = pl.ds(pl.multiple_of(soil * (chunk + BLOCK), BLOCK), chunk)
        for_keys = for_keys + mm(sides[e][:, 2 * part :], home_parts[rows, :], TN)
        block = columns_of(soil, BLOCK)
        right = jnp.concatenate([backs[d][block, :] for d in range(HEADS)], axis=0)
        for_queries = for_queries + mm(sides[e][:, :part], right[:, DH:], TN)
        for_output = for_output + mm(sides[e][:, part : 2 * part], right[:, :DH], TN)
    inner[:, : 2 * DH] = for_keys.astype(BF16)
    inner[:, 2 * DH :] = for_queries.astype(BF16)
    outer[...] = for_output.astype(BF16)


def weights_of(place, home_parts, backs, sides):
    part = sides[0].shape[1] // 3
    return call(
        weights_kernel,
        [shape(part, 3 * DH), shape(part, DH)],
        (place, home_parts, *backs, *sides),
        8 * HEADS * sides[0].shape[0] * part * DH,
    )


def home_kernel(parts, w_query, w_key, w_value, w_out, key_grad, output, query_grad):
    count = key_grad.shape[0]
    chunks = [parts.at[h * (count + BLOCK) : (h + 1) * (count + BLOCK), :] for h in range(HEADS)]
    keys = jnp.concatenate([x[:count, :DH] for x in chunks], axis=1)
    values = jnp.concatenate([x[:count, DH:] for x in chunks], axis=1)
    key_grad[...] = (mm(keys, w_key[...], NT) + mm(values, w_value[...], NT)).astype(BF16)
    attended = jnp.concatenate([x[count:, :DH] for x in chunks], axis=1)
    output[...] = mm(attended, w_out[...], NN).astype(BF16)
    grad = jnp.concatenate([x[count:, DH:] for x in chunks], axis=1)
    query_grad[...] = mm(grad, w_query[...], NT).astype(BF16)


def home_outputs(parts, w_in, w_out):
    width = w_in.shape[0]
    count = parts.shape[0] // HEADS - BLOCK
    return call(
        home_kernel,
        [shape(count, width), shape(BLOCK, width), shape(BLOCK, width)],
        (parts, w_in, w_in, w_in, w_out),
        4 * (count + BLOCK) * width * WIDTH,
        in_specs=[whole(parts), third(w_in, 0), third(w_in, 1), third(w_in, 2), whole(w_out)],
    )


def place_weights_kernel(place, *refs):
    inner, outer, (w_in_grad, w_out_grad) = refs[:HEADS], refs[HEADS : 2 * HEADS], refs[2 * HEADS :]
    rows = inner[0].shape[0]
    for d in range(HEADS):
        index = lax.rem(place[0] - d + HEADS, HEADS)
        w_in_grad[:, columns_of(index, DH)] = inner[d][:, 2 * DH :].astype(F32)
        w_in_grad[:, columns_of(HEADS + index, DH)] = inner[d][:, :DH].astype(F32)
        w_in_grad[:, columns_of(2 * HEADS + index, DH)] = inner[d][:, DH : 2 * DH].astype(F32)
        w_out_grad[:, columns_of(index, rows)] = jnp.transpose(outer[d][...].astype(F32))


def place_weights(place, inner, outer):
    rows = inner[0].shape[0]
    return call(
        place_weights_kernel,
        [shape(rows, 3 * WIDTH, F32), shape(DH, HEADS * rows, F32)],
        (place, *inner, *outer),
        rows * 4 * WIDTH,
    )


def finish_kernel(place, *refs):
    pieces, refs = refs[: 2 * HEADS], refs[2 * HEADS :]
    home, (w_in_grad, w_out_grad) = (*refs[:5], *refs[7:]), refs[5:7]
    home_kernel(*home)
    place_weights_kernel(place, *pieces, w_in_grad, w_out_grad)


def finish(place, inner, outer, parts, w_in, w_out):
    rows = inner[0].shape[0]
    width = w_in.shape[0]
    count = parts.shape[0] // HEADS - BLOCK
    return call(
        finish_kernel,
        [
            shape(rows, 3 * WIDTH, F32),
            shape(DH, HEADS * rows, F32),
            shape(count, width),
            shape(BLOCK, width),
            shape(BLOCK, width),
        ],
        (place, *inner, *outer, parts, w_in, w_in, w_in, w_out),
        4 * (count + BLOCK) * width * WIDTH,
        in_specs=[SMEM]
        + [whole(x) for x in (*inner, *outer, parts)]
        + [third(w_in, 0), third(w_in, 1), third(w_in, 2), whole(w_out)],
    )


def after(value, *others):
    return lax.optimization_barrier((value, *others))[0]


def swapped(block, axis):
    return lax.all_to_all(block, axis, 0, 0, tiled=True)


def spread_to(block, axis):
    return [block] + [sent(block, axis, d) for d in range(1, HEADS)]


def head_body(query_tokens, key_tokens, w_in, w_out, out_grad, crossing, home):
    place = None
    distances = range(1, HEADS)
    packs, slices, kvs = project(place, query_tokens, key_tokens, out_grad, w_in, w_out, crossing, home)
    packs = swapped(packs, "soil")
    kvs = [kvs[0]] + [sent(kvs[d], "soil", d) for d in distances]
    slices = [slices[0]] + [sent(slices[d], "stand", d) for d in distances]
    planes = spread_to(packs, "stand")
    side = joined(place, key_tokens, slices)
    sides = [side, sent(side, "soil", 1), sent(after(side, planes[1]), "soil", 2), sent(side, "soil", 3)]
    (back_0,), even = plane_attention(place, planes[:1], kvs)
    (back_1, back_3), odd = plane_attention(place, [planes[1], planes[3]], kvs)
    back_2, home_parts = last_attention(place, planes[2], kvs, even, odd, back_0)
    inner, outer = weights_of(place, home_parts, [back_0, back_1, back_2, back_3], sides)
    home_parts = swapped(home_parts, "soil")
    outer = spread_to(outer, "stand")
    crosswise = []
    for d in range(HEADS):
        route = [
            (soil * HEADS + stand, stand * HEADS + (soil + d) % HEADS)
            for stand in range(HEADS)
            for soil in range(HEADS)
        ]
        held = inner if d < 2 else after(inner, outer[d - 1])
        crosswise.append(lax.ppermute(held, ("soil", "stand"), route))
    results = finish(place, crosswise, outer, home_parts, w_in, w_out)
    w_in_grad, w_out_grad, key_grad, output, query_grad = results
    return (output, query_grad, key_grad, w_in_grad, w_out_grad)


NEG = -1e30


def from_behind(block, axis, distance):
    devices = range(lax.axis_size(axis))
    route = [((i - distance) % len(devices), i) for i in devices]
    return lax.ppermute(block, axis, route)


def tile_mask(allowed, offset, columns):
    key_blocks = allowed.shape[1]
    column_block = (offset + jnp.arange(columns, dtype=jnp.int32)) // BLOCK
    onehot = (jnp.arange(key_blocks, dtype=jnp.int32)[:, None] == column_block[None, :]).astype(
        jnp.float32
    )
    coarse = jnp.dot(allowed, onehot)
    expanded = jnp.broadcast_to(coarse[:, None, :], (coarse.shape[0], BLOCK, columns))
    return expanded.reshape(coarse.shape[0] * BLOCK, columns)


def guarded_update(update, allowed_mask, operands, carried):
    return update(*operands, allowed_mask, carried)


def forward_tile(queries, key_proj, values, allowed_mask, carried):
    row_best, row_total, summed = carried
    query_count = queries.shape[0]
    key_count = key_proj.shape[0]
    query_heads = queries.reshape(query_count, HEADS, DH)
    key_heads = key_proj.reshape(key_count, HEADS, DH)
    value_heads = values.reshape(key_count, HEADS, DH)
    scores = jnp.einsum(
        "qhd,khd->hqk", query_heads, key_heads, preferred_element_type=jnp.float32
    ) * (1.0 / math.sqrt(DH))
    guarded = jnp.where(allowed_mask[None, :, :] > 0, scores, NEG)
    new_best = jnp.maximum(row_best, jnp.max(guarded, axis=2))
    rescale = jnp.exp(row_best - new_best)
    weights = jnp.exp(guarded - new_best[:, :, None]) * allowed_mask[None, :, :]
    row_total = row_total * rescale + jnp.sum(weights, axis=2)
    contrib = jnp.einsum(
        "hqk,khd->qhd",
        weights.astype(jnp.bfloat16),
        value_heads,
        preferred_element_type=jnp.float32,
    )
    summed = summed.reshape(query_count, HEADS, DH) * rescale.T[:, :, None] + contrib
    return (new_best, row_total, summed.reshape(query_count, HEADS * DH))


def backward_tile(queries, grad_att, log_total, spread, key_proj, values, allowed_mask, carried):
    grad_query, grad_key, grad_value = carried
    query_count = queries.shape[0]
    key_count = key_proj.shape[0]
    query_heads = queries.reshape(query_count, HEADS, DH)
    grad_heads = grad_att.reshape(query_count, HEADS, DH)
    key_heads = key_proj.reshape(key_count, HEADS, DH)
    value_heads = values.reshape(key_count, HEADS, DH)
    score_scale = 1.0 / math.sqrt(DH)
    scores = (
        jnp.einsum("qhd,khd->hqk", query_heads, key_heads, preferred_element_type=jnp.float32)
        * score_scale
    )
    probs = jnp.exp(jnp.where(allowed_mask[None, :, :] > 0, scores - log_total[:, :, None], NEG))
    grad_probs = jnp.einsum(
        "qhd,khd->hqk", grad_heads, value_heads, preferred_element_type=jnp.float32
    )
    grad_scores = (probs * (grad_probs - spread[:, :, None])).astype(jnp.bfloat16)
    query_step = (
        jnp.einsum("hqk,khd->qhd", grad_scores, key_heads, preferred_element_type=jnp.float32)
        * score_scale
    )
    key_step = (
        jnp.einsum("hqk,qhd->khd", grad_scores, query_heads, preferred_element_type=jnp.float32)
        * score_scale
    )
    value_step = jnp.einsum(
        "hqk,qhd->khd", probs.astype(jnp.bfloat16), grad_heads, preferred_element_type=jnp.float32
    )
    grad_query = grad_query + query_step.reshape(query_count, HEADS * DH)
    grad_key = grad_key + key_step.reshape(key_count, HEADS * DH)
    grad_value = grad_value + value_step.reshape(key_count, HEADS * DH)
    return (grad_query, grad_key, grad_value)


def ring_body(query_tokens, key_tokens, w_in, w_out, out_grad, crossing, home):
    attn_width = HEADS * DH
    query_count = query_tokens.shape[0]
    key_count = key_tokens.shape[0]
    soil_count = lax.axis_size("soil")
    soil_index = lax.axis_index("soil")
    stand_count = lax.axis_size("stand")
    stand_index = lax.axis_index("stand")
    total_blocks = key_count * soil_count // BLOCK
    allowed = (
        (crossing > 0) | (home[:, None] == jnp.arange(total_blocks, dtype=jnp.int32)[None, :])
    ).astype(jnp.float32)
    queries = jnp.dot(
        query_tokens, w_in[:, :attn_width], preferred_element_type=jnp.float32
    ).astype(jnp.bfloat16)
    projected = jnp.dot(
        key_tokens, w_in[:, attn_width:], preferred_element_type=jnp.float32
    ).astype(jnp.bfloat16)
    key_proj = projected[:, :attn_width]
    values = projected[:, attn_width:]
    key_offset = soil_index * key_count
    start_state = (
        jnp.full((HEADS, query_count), NEG, jnp.float32),
        jnp.zeros((HEADS, query_count), jnp.float32),
        jnp.zeros((query_count, attn_width), jnp.float32),
    )

    def forward_turn(turn_index, carried):
        moving, running = carried
        allowed_mask = tile_mask(moving[1].astype(jnp.float32), key_offset, key_count)
        running = guarded_update(forward_tile, allowed_mask, (moving[0], key_proj, values), running)
        moving = from_behind((moving[0], moving[1]), "soil", 1)
        running = from_behind(running, "soil", 1)
        return (moving, running)

    moving, running = lax.fori_loop(
        0, soil_count, forward_turn, ((queries, allowed.astype(jnp.bfloat16)), start_state)
    )
    row_best, row_total, summed = running
    attended = (
        (summed.reshape(query_count, HEADS, DH) / row_total.T[:, :, None])
        .reshape(query_count, attn_width)
        .astype(jnp.bfloat16)
    )
    log_total = row_best + jnp.log(row_total)
    output = jnp.dot(attended, w_out, preferred_element_type=jnp.float32).astype(jnp.bfloat16)
    grad_attended = lax.dot_general(
        out_grad, w_out, (((1,), (1,)), ((), ())), preferred_element_type=jnp.float32
    ).astype(jnp.bfloat16)
    spread = jnp.sum(
        (grad_attended.astype(jnp.float32) * attended.astype(jnp.float32)).reshape(
            query_count, HEADS, DH
        ),
        axis=2,
    ).T
    zero_query = jnp.zeros((query_count, attn_width), jnp.float32)
    zero_key = jnp.zeros((key_count, attn_width), jnp.float32)

    def backward_turn(turn_index, carried):
        moving, query_stats, grad_key, grad_value = carried
        allowed_mask = tile_mask(moving[2].astype(jnp.float32), key_offset, key_count)
        grad_query, grad_key, grad_value = guarded_update(
            backward_tile,
            allowed_mask,
            (moving[0], moving[1], query_stats[0], query_stats[1], key_proj, values),
            (query_stats[2], grad_key, grad_value),
        )
        moving = from_behind((moving[0], moving[1], moving[2]), "soil", 1)
        query_stats = from_behind((query_stats[0], query_stats[1], grad_query), "soil", 1)
        return (moving, query_stats, grad_key, grad_value)

    moving, query_stats, grad_key, grad_value = lax.fori_loop(
        0,
        soil_count,
        backward_turn,
        (
            (queries, grad_attended, allowed.astype(jnp.bfloat16)),
            (log_total, spread, zero_query),
            zero_key,
            zero_key,
        ),
    )
    grad_query = query_stats[2]
    grad_key, grad_value = lax.psum((grad_key, grad_value), "stand")
    key_grad_in = jnp.concatenate([grad_key, grad_value], axis=1).astype(jnp.bfloat16)
    query_grad_in = grad_query.astype(jnp.bfloat16)
    query_grad = lax.dot_general(
        query_grad_in,
        w_in[:, :attn_width],
        (((1,), (1,)), ((), ())),
        preferred_element_type=jnp.float32,
    ).astype(jnp.bfloat16)
    key_grad = lax.dot_general(
        key_grad_in,
        w_in[:, attn_width:],
        (((1,), (1,)), ((), ())),
        preferred_element_type=jnp.float32,
    ).astype(jnp.bfloat16)
    stand_rows = key_count // stand_count
    key_slice = lax.dynamic_slice_in_dim(key_tokens, stand_index * stand_rows, stand_rows, 0)
    grad_slice = lax.dynamic_slice_in_dim(key_grad_in, stand_index * stand_rows, stand_rows, 0)
    query_part = lax.dot_general(
        query_tokens, query_grad_in, (((0,), (0,)), ((), ())), preferred_element_type=jnp.float32
    )
    key_part = lax.dot_general(
        key_slice, grad_slice, (((0,), (0,)), ((), ())), preferred_element_type=jnp.float32
    )
    w_in_part = lax.psum_scatter(
        jnp.concatenate([query_part, key_part], axis=1), "soil", scatter_dimension=0, tiled=True
    )
    w_out_part = lax.psum_scatter(
        lax.dot_general(
            attended, out_grad, (((0,), (0,)), ((), ())), preferred_element_type=jnp.float32
        ),
        "soil",
        scatter_dimension=0,
        tiled=True,
    )
    w_in_grad, w_out_grad = lax.psum((w_in_part, w_out_part), "stand")
    return (output, query_grad, key_grad, w_in_grad, w_out_grad)


def solution(mesh):
    in_specs = (
        P(("field", "stand", "soil"), None),
        P(("field", "soil"), None),
        P(),
        P(),
        P(("field", "stand", "soil"), None),
        P(("field", "stand", "soil"), None),
        P(("field", "stand", "soil")),
    )
    out_specs = (
        P(("field", "stand", "soil"), None),
        P(("field", "stand", "soil"), None),
        P(("field", "soil"), None),
        P(("field", "soil"), None),
        P(("field", "soil"), None),
    )
    square = mesh.shape["stand"] == HEADS and mesh.shape["soil"] == HEADS
    body = head_body if square else ring_body
    return jax.shard_map(body, mesh=mesh, in_specs=in_specs, out_specs=out_specs, check_vma=False)
```
